256 devices in a mesh: dp: 16 (over y, x), expert: 16 (over z, core).
Axes of the slice: x: 4, y: 4, z: 8, core: 2. Of those that a mesh axis runs over, the one named last changes fastest.
Arguments:
- tokens: bfloat16 [16384, 2048], P(('dp', 'expert')), may hold values from -6 to 6
- expert_ids: int32 [16384, 8], P(('dp', 'expert')), may hold values from 0 to 127, all different within a row; in each aligned block of 32 rows (0 to 31, 32 to 63, ...) at most 3 rows name the same one
- gate_fixed: int32 [16384, 8], P(('dp', 'expert')), may hold values from 1 to 65535
- w_gate: bfloat16 [256, 2048, 384], P(('dp', 'expert')), may hold values from -0.125 to 0.125
- w_up: bfloat16 [256, 2048, 384], P(('dp', 'expert')), may hold values from -0.125 to 0.125
- w_down: bfloat16 [256, 384, 2048], P(('dp', 'expert')), may hold values from -0.21875 to 0.21875
Outputs:
- mixed: float32 [16384, 2048], P(('dp', 'expert'))
The draws below stay inside these ranges and needn't reach their ends.
Inputs may be any that keep to these rules, and one draw needn't show every extreme that they name: `expert_ids`: each row names 8 different experts. In each aligned block of 32 rows (the first or the second half of one device's rows) no expert is named by more than 3 rows, a bound that some block reaches.
All inputs are finite; a program needn't handle non-finite values.
Results may differ from the reference program's by a relative error of at most 0.0041.
Values may be sent and summed in bfloat16 or wider, within the bound.
No kernel may reach another device: no remote copies, remote signals or barrier semaphores. Data moves between devices by JAX's collectives and lax.ppermute only.
A program may use at most 64 MiB of HBM per device.

```python
import math
import jax
import jax.numpy as jnp
import numpy as np
from jax import lax

D = 2048
FF = 768
TOP = 8
TOK_DEV = 64
HALF_FF = 384
EXPERTS = 128
CAP = 3
TOKENS = 16384


def with_ends(array, stream_key, low, top_value):
    shape = array.shape
    place = [jax.random.randint(jax.random.fold_in(stream_key, axis), (), 0, shape[axis]) for axis in range(len(shape))]
    array = array.at[tuple(place)].set(low)
    longest = shape.index(max(shape))
    place[longest] = (place[longest] + 1) % shape[longest]
    return array.at[tuple(place)].set(top_value)


def block_scale(key, extent, split, smallest, high):
    def one(axis_at, shards_of):
        steps = jax.random.uniform(jax.random.fold_in(jax.random.fold_in(key, 6), axis_at), (shards_of,), jnp.float32, smallest / len(split), high / len(split))
        return jnp.repeat(jnp.exp(steps), extent[axis_at] // shards_of).reshape((-1,) + (1,) * (len(extent) - axis_at - 1))

    loudness = one(*split[0])
    for cut in split[1:]:
        loudness = loudness * one(*cut)
    return loudness


def routed_block(rng, own, number, rows, amount, top, bound, lean):
    sequence = jax.random.permutation(rng, amount)
    heavy_load, usual = load_shares(amount, rows * top, bound, lean, True), load_shares(amount, rows * top, bound, lean, False)
    places = jnp.arange(amount)

    def named(lengths, offset_by):
        used = int((lengths > 0).sum())
        fixed = max(1, used // 4)
        shifted = fixed + (places - fixed + offset_by * (used - fixed)) % max(1, amount - fixed)
        return jnp.zeros((amount,), jnp.int32).at[sequence[jnp.where(places < fixed, places, shifted)]].set(jnp.asarray(lengths, jnp.int32))

    lengths = jnp.where(number % 4 == 0, named(heavy_load, number // 4), named(usual, number - number // 4 - 1))
    mixed = jax.random.permutation(jax.random.fold_in(own, 3), amount)
    source_of, taker = mixed[0:amount // 2 * 2:2], mixed[1:amount // 2 * 2:2]
    margin = jnp.minimum(lengths[source_of] - 1, bound - lengths[taker]) // 2
    margin = jnp.where((source_of == sequence[0]) | (taker == sequence[0]) | (lengths[taker] == 0), 0, jnp.maximum(margin, 0))
    shifted = jax.random.randint(jax.random.fold_in(own, 4), (amount // 2,), 0, 1 << 20) % (margin + 1)
    lengths = lengths.at[source_of].add(-shifted).at[taker].add(shifted)
    members = jnp.searchsorted(jnp.cumsum(lengths), jnp.arange(rows * top), side="right").astype(jnp.int32)
    table = members.reshape(top, rows).T
    table = table[jax.random.permutation(jax.random.fold_in(own, 1), rows)]
    offset_by = jax.random.randint(jax.random.fold_in(own, 2), (rows, 1), 0, top)
    return jnp.take_along_axis(table, (jnp.arange(top)[None, :] + offset_by) % top, axis=1)


def load_shares(count, total, most, slope, full):
    weights = [(1 << 20) // math.isqrt(rank ** slope) + 1 for rank in range(1, count + 1)]
    largest = most if full else min(most, max(-(-total // count), total * weights[0] // sum(weights)))
    least = 1 if total - largest >= count - 1 else 0
    given, rest = [largest] + [least] * (count - 1), total - largest - least * (count - 1)
    while rest > 0:
        candidates = [i for i in range(1, count) if given[i] < largest] or [i for i in range(1, count) if given[i] < most]
        whole, left = sum([weights[i] for i in candidates]), rest
        for i in candidates:
            addition = min(most - given[i], max(1, left * weights[i] // whole), rest)
            given[i] = given[i] + addition
            rest = rest - addition
    return np.array(given)


def gaussian(key, extent, deviation, limit, cuts=(), kind=jnp.bfloat16):
    values = jax.random.normal(key, extent, jnp.float32) * deviation
    if len(cuts) > 0:
        values = block_scale(key, extent, cuts, -0.22, 0.18) * values
    return jnp.clip(values, min=-limit, max=limit).astype(kind)


def setup_inputs(seed: int = 0) -> dict:
    streams_of = jax.random.split(jax.random.key(seed), 7)
    tokens = gaussian(streams_of[0], (TOKENS, D), 1.0, 6.0, ((0, 256),))
    expert_ids_keys = jax.random.split(jax.random.fold_in(streams_of[1], 1), TOKENS // (TOK_DEV // 2))
    expert_ids_turns = jax.random.permutation(jax.random.fold_in(streams_of[1], 3), TOKENS // (TOK_DEV // 2))
    expert_ids = jax.vmap(lambda own, number: routed_block(jax.random.fold_in(streams_of[1], 2), own, number, TOK_DEV // 2, EXPERTS, TOP, CAP, 2))(expert_ids_keys, expert_ids_turns).reshape((TOKENS, TOP))
    gate_fixed = with_ends(jax.random.randint(streams_of[2], (TOKENS, TOP), 1, 65536), jax.random.fold_in(streams_of[2], 1), 1, 65535).astype(jnp.int32)
    w_gate = gaussian(streams_of[3], (2 * EXPERTS, D, HALF_FF), D ** -0.5, 0.125, ((0, 256),))
    w_up = gaussian(streams_of[4], (2 * EXPERTS, D, HALF_FF), D ** -0.5, 0.125, ((0, 256),))
    w_down = gaussian(streams_of[5], (2 * EXPERTS, HALF_FF, D), FF ** -0.5, 0.21875, ((0, 256),))
    return {"tokens": tokens, "expert_ids": expert_ids, "gate_fixed": gate_fixed, "w_gate": w_gate, "w_up": w_up, "w_down": w_down}


def reference(tokens, expert_ids, gate_fixed, w_gate, w_up, w_down):
    tile_rows = 256
    gates = gate_fixed.astype(jnp.float32)
    mix_weight = gates / jnp.sum(gates, axis=1, keepdims=True)
    mix_flat = mix_weight.reshape(-1)
    flat_ids = expert_ids.reshape(-1).astype(jnp.int32)
    order_idx = jnp.argsort(flat_ids, stable=True).astype(jnp.int32)
    counts = jnp.bincount(flat_ids, length=EXPERTS).astype(jnp.int32)
    starts = (jnp.cumsum(counts) - counts).astype(jnp.int32)
    order_pad = jnp.concatenate([order_idx, jnp.zeros((tile_rows,), jnp.int32)])
    positions = jnp.arange(tile_rows, dtype=jnp.int32)

    def per_expert(total, expert_index):
        wg_full = jnp.concatenate([w_gate[2 * expert_index], w_gate[2 * expert_index + 1]], axis=1)
        wu_full = jnp.concatenate([w_up[2 * expert_index], w_up[2 * expert_index + 1]], axis=1)
        wd_full = jnp.concatenate([w_down[2 * expert_index], w_down[2 * expert_index + 1]], axis=0)
        count = counts[expert_index]
        begin = starts[expert_index]
        steps_needed = (count + tile_rows - 1) // tile_rows

        def tile_step(tile_index, accum):
            offset = (tile_index * tile_rows).astype(jnp.int32)
            picked = lax.dynamic_slice(order_pad, ((begin + offset).astype(jnp.int32),), (tile_rows,))
            valid = (offset + positions) < count
            token_index = picked // TOP
            token_rows = tokens[token_index]
            gate_part = jnp.dot(token_rows, wg_full, preferred_element_type=jnp.float32)
            up_part = jnp.dot(token_rows, wu_full, preferred_element_type=jnp.float32)
            hidden = (jax.nn.silu(gate_part) * up_part).astype(jnp.bfloat16)
            expert_out = jnp.dot(hidden, wd_full, preferred_element_type=jnp.float32).astype(jnp.bfloat16)
            weight = jnp.where(valid, mix_flat[picked], jnp.zeros((), jnp.float32))
            return accum.at[token_index].add(weight[:, None] * expert_out.astype(jnp.float32))

        return lax.fori_loop(jnp.int32(0), steps_needed.astype(jnp.int32), tile_step, total), None

    mixed, _ = lax.scan(per_expert, jnp.zeros((TOKENS, D), jnp.float32), jnp.arange(EXPERTS, dtype=jnp.int32))
    return mixed
```

```python
import functools

import jax
import jax.numpy as jnp
from jax import lax
from jax.experimental import pallas as pl
from jax.experimental.pallas import tpu as pltpu
from jax.sharding import PartitionSpec as P

F32 = jnp.float32
BF16 = jnp.bfloat16
EXTRA = 128
VMEM = pl.BlockSpec(memory_space=pltpu.VMEM)
SMEM = pl.BlockSpec(memory_space=pltpu.SMEM)
PARAMS = pltpu.CompilerParams(vmem_limit_bytes=56 << 20)


def slot_of(index, slots):
    group = jnp.zeros_like(index)
    for d in range(1, 16):
        group = group + (index >= d * slots).astype(jnp.int32)
    return group, index - group * slots


def dispatch_kernel(slots, planes, z_ref, x_ref, out_ref):
    tokens = x_ref.shape[0]
    width = out_ref.shape[1]
    groups = out_ref.shape[0] // slots
    extra = x_ref[:, width:].astype(F32).T
    dest = planes * lax.broadcasted_iota(jnp.int32, (groups, 1), 0) + z_ref[0]
    dest = dest.astype(F32)
    match = jnp.zeros((groups, tokens), F32)
    for k in range(8):
        match = match + (extra[k : k + 1, :] == dest).astype(F32)
    upper = lax.broadcasted_iota(jnp.int32, (tokens, tokens), 0) <= lax.broadcasted_iota(
        jnp.int32, (tokens, tokens), 1
    )
    upper = upper.astype(F32).astype(BF16)
    order = jnp.dot(match.astype(BF16), upper, preferred_element_type=F32) * match
    row = lax.broadcasted_iota(jnp.int32, (groups * slots, 1), 0)
    group, place = slot_of(row, slots)
    spread = (group == lax.broadcasted_iota(jnp.int32, (1, groups), 1)).astype(F32).astype(BF16)
    wanted = jnp.dot(spread, order.astype(BF16), preferred_element_type=F32)
    pick = (wanted == (place + 1).astype(F32)).astype(F32).astype(BF16)
    out_ref[...] = jnp.dot(pick, x_ref[:, :width], preferred_element_type=F32).astype(BF16)


def expert_kernel(x_ref, g0, g1, u0, u1, d0, d1, out_ref):
    rows = x_ref.shape[0]
    step = 256
    for r in range(0, rows, step):
        x = x_ref[r : r + step, :]
        total = None
        for g_ref, u_ref, d_ref in ((g0, u0, d0), (g1, u1, d1)):
            gate = jnp.dot(x, g_ref[...], preferred_element_type=F32)
            up = jnp.dot(x, u_ref[...], preferred_element_type=F32)
            hidden = (gate / (1.0 + jnp.exp(-gate)) * up).astype(BF16)
            part = jnp.dot(hidden, d_ref[...], preferred_element_type=F32)
            total = part if total is None else total + part
        out_ref[r : r + step, :] = total.astype(BF16)


def combine_kernel(slots, planes, z_ref, extra_ref, home_ref, out_ref):
    tokens = extra_ref.shape[0]
    groups = home_ref.shape[0] // slots
    extra = extra_ref[...].astype(F32)
    gates = extra[:, 8:16] * 256.0 + extra[:, 16:24]
    mix = gates / jnp.sum(gates, axis=1, keepdims=True)
    dest = planes * lax.broadcasted_iota(jnp.int32, (1, EXTRA), 1) + z_ref[0]
    dest = dest.astype(F32)
    match = jnp.zeros((tokens, EXTRA), F32)
    weight = jnp.zeros((tokens, EXTRA), F32)
    for k in range(8):
        same = extra[:, k : k + 1] == dest
        match = match + same.astype(F32)
        weight = weight + jnp.where(same, mix[:, k : k + 1], 0.0)
    lower = lax.broadcasted_iota(jnp.int32, (tokens, tokens), 1) <= lax.broadcasted_iota(
        jnp.int32, (tokens, tokens), 0
    )
    lower = lower.astype(F32).astype(BF16)
    order = jnp.dot(lower, match.astype(BF16), preferred_element_type=F32) * match
    column = lax.broadcasted_iota(jnp.int32, (1, groups * slots), 1)
    group, place = slot_of(column, slots)
    spread = (group == lax.broadcasted_iota(jnp.int32, (EXTRA, 1), 0)).astype(F32).astype(BF16)
    wanted = jnp.dot(order.astype(BF16), spread, preferred_element_type=F32)
    here = wanted == (place + 1).astype(F32)
    high = weight.astype(BF16)
    low = (weight - high.astype(F32)).astype(BF16)
    home = home_ref[...]
    total = None
    for piece in (high, low):
        wide = jnp.dot(piece, spread, preferred_element_type=F32)
        wide = jnp.where(here, wide, 0.0).astype(BF16)
        part = jnp.dot(wide, home, preferred_element_type=F32)
        total = part if total is None else total + part
    out_ref[...] = total


def per_device(tokens, expert_ids, gate_fixed, w_gate, w_up, w_down):
    col_count = lax.axis_size("expert")
    dp_count = lax.axis_size("dp")
    planes = col_count // 2
    rows, width = tokens.shape
    block = 3 * rows // 32
    slots = block * planes // 2
    plane = (lax.axis_index("expert") // 2).astype(jnp.int32).reshape(1)

    def along_z(x, by):
        return lax.ppermute(
            x, "expert", [(i, (i + 2 * by) % col_count) for i in range(col_count)]
        )

    def partner(x):
        return lax.ppermute(x, "expert", [(i, i ^ 1) for i in range(col_count)])

    packed = jnp.concatenate(
        [expert_ids, gate_fixed // 256, gate_fixed % 256, jnp.zeros((rows, EXTRA - 24), jnp.int32)],
        axis=1,
    ).astype(BF16)
    mine = jnp.concatenate([tokens, packed], axis=1)
    half = planes // 2
    up = down = mine
    shards = [mine]
    for step in range(half):
        up = along_z(up, 1)
        shards.append(up)
        if step < half - 1:
            down = along_z(down, -1)
            shards.append(down)
    gathered = jnp.concatenate(shards, axis=0)
    weights = []
    for w in (w_gate[0], w_up[0], w_down[0]):
        weights += [w, partner(w)]

    slots = 3 * planes * rows // 32
    outgoing = pl.pallas_call(
        functools.partial(dispatch_kernel, slots, planes),
        out_shape=jax.ShapeDtypeStruct((dp_count * slots, width), BF16),
        in_specs=[SMEM, VMEM],
        out_specs=VMEM,
        compiler_params=PARAMS,
        name="dispatch",
    )(plane, gathered)
    arrived = lax.all_to_all(outgoing, "dp", split_axis=0, concat_axis=0, tiled=True)
    expert_out = pl.pallas_call(
        expert_kernel,
        out_shape=jax.ShapeDtypeStruct(arrived.shape, BF16),
        in_specs=[VMEM] * 7,
        out_specs=VMEM,
        compiler_params=PARAMS,
        name="expert",
    )(arrived, *weights)
    home = lax.all_to_all(expert_out, "dp", split_axis=0, concat_axis=0, tiled=True)
    partial = pl.pallas_call(
        functools.partial(combine_kernel, slots, planes),
        out_shape=jax.ShapeDtypeStruct((planes * rows, width), F32),
        in_specs=[SMEM, VMEM, VMEM],
        out_specs=VMEM,
        compiler_params=PARAMS,
        name="combine",
    )(plane, gathered[:, width:], home)

    part = [partial[i * rows : (i + 1) * rows] for i in range(planes)]
    from_low = [part[2 * i - 1] for i in range(1, half + 1)]
    from_high = [part[2 * i] for i in range(1, half)]
    down = from_low[half - 1].astype(BF16)
    up = from_high[half - 2].astype(BF16)
    for step in range(half):
        down = along_z(down, -1)
        if step < half - 1:
            down = (down.astype(F32) + from_low[half - 2 - step]).astype(BF16)
            up = along_z(up, 1)
            if step < half - 2:
                up = (up.astype(F32) + from_high[half - 3 - step]).astype(BF16)
    return part[0] + up.astype(F32) + down.astype(F32)


def solution(mesh):
    rows = P(("dp", "expert"), None)
    panels = P(("dp", "expert"), None, None)
    return jax.shard_map(
        per_device,
        mesh=mesh,
        in_specs=(rows, rows, rows, panels, panels, panels),
        out_specs=rows,
        check_vma=False,
    )
```

```python
import functools

import jax
import jax.numpy as jnp
from jax import lax
from jax.experimental import pallas as pl
from jax.experimental.pallas import tpu as pltpu
from jax.sharding import PartitionSpec as P

F32 = jnp.float32
BF16 = jnp.bfloat16
EXTRA = 128
VMEM = pl.BlockSpec(memory_space=pltpu.VMEM)
SMEM = pl.BlockSpec(memory_space=pltpu.SMEM)
PARAMS = pltpu.CompilerParams(vmem_limit_bytes=20 << 20)


def on_chip(x):
    return pltpu.with_memory_space_constraint(x, pltpu.VMEM)


def after(x, *others):
    return lax.optimization_barrier((x,) + others)[0]


def kernel_call(body, name, outs, arrays, scalars=(), keep=False):
    return pl.pallas_call(
        body,
        out_shape=[pltpu.VMEM(*out) if keep else jax.ShapeDtypeStruct(*out) for out in outs],
        in_specs=[SMEM] * len(scalars) + [VMEM] * len(arrays),
        out_specs=[VMEM] * len(outs),
        compiler_params=PARAMS,
        name=name,
    )(*scalars, *arrays)


def slot_of(index, slots):
    group = jnp.zeros_like(index)
    for d in range(1, 16):
        group = group + (index >= d * slots).astype(jnp.int32)
    return group, index - group * slots


def dispatch_kernel(slots, planes, z_ref, *refs):
    refs, out_ref, extra_ref = refs[:-2], refs[-2], refs[-1]
    width = out_ref.shape[1]
    groups = out_ref.shape[0] // slots
    extra = jnp.concatenate([x[:, width:] for x in refs], axis=0)
    extra_ref[...] = extra
    extra = extra.astype(F32).T
    tokens = extra.shape[1]
    dest = planes * lax.broadcasted_iota(jnp.int32, (groups, 1), 0) + z_ref[0]
    dest = dest.astype(F32)
    match = jnp.zeros((groups, tokens), F32)
    for k in range(8):
        match = match + (extra[k : k + 1, :] == dest).astype(F32)
    upper = lax.broadcasted_iota(jnp.int32, (tokens, tokens), 0) <= lax.broadcasted_iota(
        jnp.int32, (tokens, tokens), 1
    )
    upper = upper.astype(F32).astype(BF16)
    order = jnp.dot(match.astype(BF16), upper, preferred_element_type=F32) * match
    row = lax.broadcasted_iota(jnp.int32, (groups * slots, 1), 0)
    group, place = slot_of(row, slots)
    spread = (group == lax.broadcasted_iota(jnp.int32, (1, groups), 1)).astype(F32).astype(BF16)
    wanted = jnp.dot(spread, order.astype(BF16), preferred_element_type=F32)
    pick = (wanted == (place + 1).astype(F32)).astype(F32).astype(BF16)
    rows = jnp.concatenate([x[:, :width] for x in refs], axis=0)
    out_ref[...] = jnp.dot(pick, rows, preferred_element_type=F32).astype(BF16)


def expert_kernel(x_ref, g0, g1, u0, u1, d0, d1, out_ref):
    x = x_ref[...]
    total = None
    for g_ref, u_ref, d_ref in ((g0, u0, d0), (g1, u1, d1)):
        gate = jnp.dot(x, g_ref[...], preferred_element_type=F32)
        up = jnp.dot(x, u_ref[...], preferred_element_type=F32)
        hidden = (gate / (1.0 + jnp.exp(-gate)) * up).astype(BF16)
        part = jnp.dot(hidden, d_ref[...], preferred_element_type=F32)
        total = part if total is None else total + part
    out_ref[...] = total.astype(BF16)


def weights_kernel(slots, planes, z_ref, extra_ref, high_ref, low_ref):
    tokens, columns = high_ref.shape
    groups = columns // slots
    extra = extra_ref[...].astype(F32)
    gates = extra[:, 8:16] * 256.0 + extra[:, 16:24]
    mix = gates / jnp.sum(gates, axis=1, keepdims=True)
    dest = planes * lax.broadcasted_iota(jnp.int32, (1, EXTRA), 1) + z_ref[0]
    dest = dest.astype(F32)
    match = jnp.zeros((tokens, EXTRA), F32)
    weight = jnp.zeros((tokens, EXTRA), F32)
    for k in range(8):
        same = extra[:, k : k + 1] == dest
        match = match + same.astype(F32)
        weight = weight + jnp.where(same, mix[:, k : k + 1], 0.0)
    lower = lax.broadcasted_iota(jnp.int32, (tokens, tokens), 1) <= lax.broadcasted_iota(
        jnp.int32, (tokens, tokens), 0
    )
    lower = lower.astype(F32).astype(BF16)
    order = jnp.dot(lower, match.astype(BF16), preferred_element_type=F32) * match
    column = lax.broadcasted_iota(jnp.int32, (1, groups * slots), 1)
    group, place = slot_of(column, slots)
    spread = (group == lax.broadcasted_iota(jnp.int32, (EXTRA, 1), 0)).astype(F32).astype(BF16)
    wanted = jnp.dot(order.astype(BF16), spread, preferred_element_type=F32)
    here = wanted == (place + 1).astype(F32)
    high = weight.astype(BF16)
    low = (weight - high.astype(F32)).astype(BF16)
    for piece, ref in ((high, high_ref), (low, low_ref)):
        wide = jnp.dot(piece, spread, preferred_element_type=F32)
        ref[...] = jnp.where(here, wide, 0.0).astype(BF16)


def combine_kernel(home_ref, high_ref, low_ref, *outs):
    home = home_ref[...]
    total = jnp.dot(high_ref[...], home, preferred_element_type=F32)
    total = total + jnp.dot(low_ref[...], home, preferred_element_type=F32)
    start = 0
    for out in outs:
        rows = out.shape[0]
        out[...] = total[start : start + rows, :].astype(out.dtype)
        start += rows


def per_device(tokens, expert_ids, gate_fixed, w_gate, w_up, w_down):
    col_count = lax.axis_size("expert")
    dp_count = lax.axis_size("dp")
    planes = col_count // 2
    half = planes // 2
    all_rows, width = tokens.shape
    rows = all_rows // 2
    slots = 3 * planes * rows // 32
    plane = (lax.axis_index("expert") // 2).astype(jnp.int32).reshape(1)

    def along_z(x, by):
        return lax.ppermute(
            x, "expert", [(i, (i + 2 * by) % col_count) for i in range(col_count)]
        )

    def partner(x):
        return lax.ppermute(x, "expert", [(i, i ^ 1) for i in range(col_count)])

    packed = jnp.concatenate(
        [
            expert_ids,
            gate_fixed // 256,
            gate_fixed % 256,
            jnp.zeros((all_rows, EXTRA - 24), jnp.int32),
        ],
        axis=1,
    ).astype(BF16)
    mine = jnp.concatenate([tokens, packed], axis=1)

    def gather(own):
        up = down = own
        shards = [own]
        for step in range(half):
            up = along_z(up, 1)
            shards.append(up)
            if step < half - 1:
                down = along_z(down, -1)
                shards.append(down)
        return shards

    def exchange(x):
        return lax.all_to_all(x, "dp", split_axis=0, concat_axis=0, tiled=True)

    def dispatch(shards):
        return kernel_call(
            functools.partial(dispatch_kernel, slots, planes),
            "dispatch",
            [((dp_count * slots, width), BF16), ((planes * rows, EXTRA), BF16)],
            [on_chip(x) for x in shards],
            [plane],
        )

    def mixing(extra):
        shape = (planes * rows, dp_count * slots)
        return kernel_call(
            functools.partial(weights_kernel, slots, planes),
            "mixing",
            [(shape, BF16), (shape, BF16)],
            [extra],
            [plane],
        )

    def scatter(part):
        from_low = [part[2 * i - 1] for i in range(1, half + 1)]
        from_high = [part[2 * i] for i in range(1, half)]
        down = from_low[half - 1]
        up = from_high[half - 2]
        marks = []
        for step in range(half):
            down = along_z(down, -1)
            if step < half - 1:
                down = (down.astype(F32) + from_low[half - 2 - step]).astype(BF16)
                up = along_z(up, 1)
                if step < half - 2:
                    up = (up.astype(F32) + from_high[half - 3 - step]).astype(BF16)
            marks.append(down)
        return part[0] + up.astype(F32) + down.astype(F32), marks

    panels = []
    for w in (w_gate[0], w_up[0], w_down[0]):
        panels += [w, partner(w)]

    def expert(x):
        return kernel_call(expert_kernel, "expert", [(x.shape, BF16)], [x] + panels)[0]

    def combine(home, mix, keep):
        kinds = [F32] * (planes - 2) + [BF16] * 2
        outs = [((rows, width), kind) for kind in kinds]
        return kernel_call(combine_kernel, "combine", outs, [home] + list(mix), keep=keep)

    first = gather(mine[:rows])
    out_0, extra_0 = dispatch(first)
    there_0 = exchange(out_0)
    second = gather(after(mine[rows:], first[-2]))
    out_1, extra_1 = dispatch(second)
    there_0 = after(there_0, out_1)
    there_1 = exchange(out_1)
    done_0 = expert(there_0)
    done_0 = after(done_0, there_1)
    home_0 = exchange(done_0)
    mix_0, mix_1 = mixing(extra_0), mixing(extra_1)
    done_1 = after(expert(there_1), *mix_0, *mix_1)
    home_1 = exchange(done_1)
    mixed_0, marks = scatter(combine(home_0, mix_0, False))
    home_1 = after(home_1, marks[half - 2])
    mixed_1, _ = scatter(combine(home_1, mix_1, True))
    return jnp.concatenate([mixed_0, mixed_1], axis=0)


def solution(mesh):
    rows = P(("dp", "expert"), None)
    panels = P(("dp", "expert"), None, None)
    return jax.shard_map(
        per_device,
        mesh=mesh,
        in_specs=(rows, rows, rows, panels, panels, panels),
        out_specs=rows,
        check_vma=False,
    )
```

```python
import functools

import jax
import jax.numpy as jnp
from jax import lax
from jax.experimental import pallas as pl
from jax.experimental.pallas import tpu as pltpu
from jax.sharding import PartitionSpec as P

F32 = jnp.float32
BF16 = jnp.bfloat16
EXTRA = 128
VMEM = pl.BlockSpec(memory_space=pltpu.VMEM)
SMEM = pl.BlockSpec(memory_space=pltpu.SMEM)
PARAMS = pltpu.CompilerParams(vmem_limit_bytes=20 << 20)


def on_chip(x):
    return pltpu.with_memory_space_constraint(x, pltpu.VMEM)


def after(x, *others):
    return lax.optimization_barrier((x,) + others)[0]


def kernel_call(body, name, outs, arrays, scalars=(), keep=False):
    return pl.pallas_call(
        body,
        out_shape=[pltpu.VMEM(*out) if keep else jax.ShapeDtypeStruct(*out) for out in outs],
        in_specs=[SMEM] * len(scalars) + [VMEM] * len(arrays),
        out_specs=[VMEM] * len(outs),
        compiler_params=PARAMS,
        name=name,
    )(*scalars, *arrays)


def slot_of(index, slots):
    group = jnp.zeros_like(index)
    for d in range(1, 16):
        group = group + (index >= d * slots).astype(jnp.int32)
    return group, index - group * slots


def dispatch_kernel(slots, planes, z_ref, *refs):
    refs, out_ref, extra_ref = refs[:-2], refs[-2], refs[-1]
    width = out_ref.shape[1]
    groups = out_ref.shape[0] // slots
    extra = jnp.concatenate([x[:, width:] for x in refs], axis=0)
    extra_ref[...] = extra
    extra = extra.astype(F32).T
    tokens = extra.shape[1]
    dest = planes * lax.broadcasted_iota(jnp.int32, (groups, 1), 0) + z_ref[0]
    dest = dest.astype(F32)
    match = jnp.zeros((groups, tokens), F32)
    for k in range(8):
        match = match + (extra[k : k + 1, :] == dest).astype(F32)
    upper = lax.broadcasted_iota(jnp.int32, (tokens, tokens), 0) <= lax.broadcasted_iota(
        jnp.int32, (tokens, tokens), 1
    )
    upper = upper.astype(F32).astype(BF16)
    order = jnp.dot(match.astype(BF16), upper, preferred_element_type=F32) * match
    row = lax.broadcasted_iota(jnp.int32, (groups * slots, 1), 0)
    group, place = slot_of(row, slots)
    spread = (group == lax.broadcasted_iota(jnp.int32, (1, groups), 1)).astype(F32).astype(BF16)
    wanted = jnp.dot(spread, order.astype(BF16), preferred_element_type=F32)
    pick = (wanted == (place + 1).astype(F32)).astype(F32).astype(BF16)
    rows = jnp.concatenate([x[:, :width] for x in refs], axis=0)
    out_ref[...] = jnp.dot(pick, rows, preferred_element_type=F32).astype(BF16)


def expert_kernel(x_ref, g0, g1, u0, u1, d0, d1, out_ref):
    x = x_ref[...]
    total = None
    for g_ref, u_ref, d_ref in ((g0, u0, d0), (g1, u1, d1)):
        gate = jnp.dot(x, g_ref[...], preferred_element_type=F32)
        up = jnp.dot(x, u_ref[...], preferred_element_type=F32)
        hidden = (gate / (1.0 + jnp.exp(-gate)) * up).astype(BF16)
        part = jnp.dot(hidden, d_ref[...], preferred_element_type=F32)
        total = part if total is None else total + part
    out_ref[...] = total.astype(BF16)


def weights_kernel(slots, planes, z_ref, extra_ref, high_ref, low_ref):
    tokens, columns = high_ref.shape
    groups = columns // slots
    extra = extra_ref[...].astype(F32)
    gates = extra[:, 8:16] * 256.0 + extra[:, 16:24]
    mix = gates / jnp.sum(gates, axis=1, keepdims=True)
    dest = planes * lax.broadcasted_iota(jnp.int32, (1, EXTRA), 1) + z_ref[0]
    dest = dest.astype(F32)
    match = jnp.zeros((tokens, EXTRA), F32)
    weight = jnp.zeros((tokens, EXTRA), F32)
    for k in range(8):
        same = extra[:, k : k + 1] == dest
        match = match + same.astype(F32)
        weight = weight + jnp.where(same, mix[:, k : k + 1], 0.0)
    lower = lax.broadcasted_iota(jnp.int32, (tokens, tokens), 1) <= lax.broadcasted_iota(
        jnp.int32, (tokens, tokens), 0
    )
    lower = lower.astype(F32).astype(BF16)
    order = jnp.dot(lower, match.astype(BF16), preferred_element_type=F32) * match
    column = lax.broadcasted_iota(jnp.int32, (1, groups * slots), 1)
    group, place = slot_of(column, slots)
    spread = (group == lax.broadcasted_iota(jnp.int32, (EXTRA, 1), 0)).astype(F32).astype(BF16)
    wanted = jnp.dot(order.astype(BF16), spread, preferred_element_type=F32)
    here = wanted == (place + 1).astype(F32)
    high = weight.astype(BF16)
    low = (weight - high.astype(F32)).astype(BF16)
    for piece, ref in ((high, high_ref), (low, low_ref)):
        wide = jnp.dot(piece, spread, preferred_element_type=F32)
        ref[...] = jnp.where(here, wide, 0.0).astype(BF16)


def combine_kernel(home_ref, high_ref, low_ref, *outs):
    home = home_ref[...]
    total = jnp.dot(high_ref[...], home, preferred_element_type=F32)
    total = total + jnp.dot(low_ref[...], home, preferred_element_type=F32)
    start = 0
    for out in outs:
        rows = out.shape[0]
        out[...] = total[start : start + rows, :].astype(out.dtype)
        start += rows


def per_device(tokens, expert_ids, gate_fixed, w_gate, w_up, w_down):
    col_count = lax.axis_size("expert")
    dp_count = lax.axis_size("dp")
    planes = col_count // 2
    half = planes // 2
    rows, width = tokens.shape
    slots = 3 * half * rows // 32
    plane = (lax.axis_index("expert") // 2).astype(jnp.int32).reshape(1)

    def along_z(x, by):
        return lax.ppermute(
            x, "expert", [(i, (i + 2 * by) % col_count) for i in range(col_count)]
        )

    def partner(x):
        return lax.ppermute(x, "expert", [(i, i ^ 1) for i in range(col_count)])

    packed = jnp.concatenate(
        [
            expert_ids,
            gate_fixed // 256,
            gate_fixed % 256,
            jnp.zeros((rows, EXTRA - 24), jnp.int32),
        ],
        axis=1,
    ).astype(BF16)
    mine = jnp.concatenate([tokens, packed], axis=1)

    def exchange(x):
        return lax.all_to_all(x, "dp", split_axis=0, concat_axis=0, tiled=True)

    def dispatch(shards):
        return kernel_call(
            functools.partial(dispatch_kernel, slots, planes),
            "dispatch",
            [((dp_count * slots, width), BF16), ((half * rows, EXTRA), BF16)],
            [on_chip(x) for x in shards],
            [plane],
        )

    def mixing(extra):
        shape = (half * rows, dp_count * slots)
        return kernel_call(
            functools.partial(weights_kernel, slots, planes),
            "mixing",
            [(shape, BF16), (shape, BF16)],
            [extra],
            [plane],
        )

    panels = []
    for w in (w_gate[0], w_up[0], w_down[0]):
        panels += [w, partner(w)]

    def expert(x):
        return kernel_call(expert_kernel, "expert", [(x.shape, BF16)], [x] + panels)[0]

    def combine(home, mix, kinds, keep):
        outs = [((rows, width), kind) for kind in kinds]
        return kernel_call(combine_kernel, "combine", outs, [home] + list(mix), keep=keep)

    def plus(x, part):
        return (x.astype(F32) + part).astype(BF16)

    low_1, high_1 = along_z(mine, 1), along_z(mine, -1)
    low_2, high_2 = along_z(low_1, 1), along_z(high_1, -1)
    low_3, high_3 = along_z(low_2, 1), along_z(high_2, -1)
    low_4 = along_z(low_3, 1)

    near_rows, near_extra = dispatch([mine, low_1, high_1, low_2])
    near = exchange(after(near_rows, high_2))
    far_rows, far_extra = dispatch([high_2, low_3, high_3, low_4])
    near = after(near, far_rows)
    far = exchange(far_rows)
    near_out = after(expert(near), far)
    near_mix, far_mix = mixing(near_extra), mixing(far_extra)
    far_out = after(expert(far), near_out, *near_mix, *far_mix)
    far_home = exchange(far_out)
    near_home = exchange(after(near_out, far_home))
    to_high_2, to_low_3, to_high_3, to_low_4 = combine(far_home, far_mix, [F32, F32, BF16, BF16], True)
    down, up = along_z(to_low_4, -1), along_z(to_high_3, 1)
    down, up = along_z(plus(down, to_low_3), -1), along_z(plus(up, to_high_2), 1)
    near_home = after(near_home, down, up)
    own, to_low_1, to_high_1, to_low_2 = combine(near_home, near_mix, [F32] * 4, True)
    down, up = along_z(plus(down, to_low_2), -1), along_z(plus(up, to_high_1), 1)
    down = along_z(plus(down, to_low_1), -1)
    return own + up.astype(F32) + down.astype(F32)


def solution(mesh):
    rows = P(("dp", "expert"), None)
    panels = P(("dp", "expert"), None, None)
    return jax.shard_map(
        per_device,
        mesh=mesh,
        in_specs=(rows, rows, rows, panels, panels, panels),
        out_specs=rows,
        check_vma=False,
    )
```

```python
import functools

import jax
import jax.numpy as jnp
from jax import lax
from jax.experimental import pallas as pl
from jax.experimental.pallas import tpu as pltpu
from jax.sharding import PartitionSpec as P

F32 = jnp.float32
BF16 = jnp.bfloat16
EXTRA = 128
VMEM = pl.BlockSpec(memory_space=pltpu.VMEM)
SMEM = pl.BlockSpec(memory_space=pltpu.SMEM)
HBM = pl.BlockSpec(memory_space=pltpu.HBM)
PIECE = 128
PARAMS = pltpu.CompilerParams(vmem_limit_bytes=24 << 20)


def on_chip(x):
    return pltpu.with_memory_space_constraint(x, pltpu.VMEM)


def off_chip(x):
    return pltpu.with_memory_space_constraint(x, pltpu.HBM)


def after(x, *others):
    return lax.optimization_barrier((x,) + others)[0]


def kernel_call(
    body, name, outs, arrays, scalars=(), keep=(), specs=None, out_specs=None, scratch=()
):
    keep = list(keep) + [jax.ShapeDtypeStruct] * (len(outs) - len(keep))
    return pl.pallas_call(
        body,
        out_shape=[where(*out) for where, out in zip(keep, outs)],
        in_specs=[SMEM] * len(scalars) + (specs or [VMEM] * len(arrays)),
        out_specs=out_specs or [VMEM] * len(outs),
        scratch_shapes=list(scratch),
        compiler_params=PARAMS,
        name=name,
    )(*scalars, *arrays)


def slot_of(index, slots):
    group = jnp.zeros_like(index)
    for d in range(1, 16):
        group = group + (index >= d * slots).astype(jnp.int32)
    return group, index - group * slots


def pack_kernel(tokens_ref, ids_ref, gates_ref, first_ref, second_ref):
    rows, width = first_ref.shape[0], tokens_ref.shape[1]
    gates = gates_ref[...]
    columns = [ids_ref[...], gates >> 8, gates & 255]
    top = jnp.concatenate(columns, axis=0).astype(F32)
    top = jnp.concatenate([top, jnp.zeros((top.shape[0], EXTRA - 2 * rows), F32)], axis=1)
    extra = jnp.concatenate([top, jnp.zeros((EXTRA - top.shape[0], EXTRA), F32)], axis=0).T
    for start, ref in ((0, first_ref), (rows, second_ref)):
        ref[:, :width] = tokens_ref[start : start + rows, :]
        ref[:, width:] = extra[start : start + rows, :].astype(BF16)


def dispatch_kernel(slots, planes, z_ref, *refs):
    refs, (out_ref, extra_ref, piece_ref, sems) = refs[:-4], refs[-4:]
    width = out_ref.shape[1]
    groups = out_ref.shape[0] // slots
    extra = jnp.concatenate([x[:, width:] for x in refs], axis=0)
    extra_ref[...] = extra
    extra = extra.astype(F32).T
    tokens = extra.shape[1]
    dest = planes * lax.broadcasted_iota(jnp.int32, (groups, 1), 0) + z_ref[0]
    dest = dest.astype(F32)
    match = jnp.zeros((groups, tokens), F32)
    for k in range(8):
        match = match + (extra[k : k + 1, :] == dest).astype(F32)
    upper = lax.broadcasted_iota(jnp.int32, (tokens, tokens), 0) <= lax.broadcasted_iota(
        jnp.int32, (tokens, tokens), 1
    )
    upper = upper.astype(F32).astype(BF16)
    order = jnp.dot(match.astype(BF16), upper, preferred_element_type=F32) * match
    row = lax.broadcasted_iota(jnp.int32, (groups * slots, 1), 0)
    group, place = slot_of(row, slots)
    spread = (group == lax.broadcasted_iota(jnp.int32, (1, groups), 1)).astype(F32).astype(BF16)
    wanted = jnp.dot(spread, order.astype(BF16), preferred_element_type=F32)
    pick = (wanted == (place + 1).astype(F32)).astype(F32).astype(BF16)
    rows = jnp.concatenate([x[:, :width] for x in refs], axis=0)
    copies = []
    for i in range(out_ref.shape[0] // PIECE):
        here = pl.ds(i * PIECE, PIECE)
        part = pick[i * PIECE : (i + 1) * PIECE, :]
        piece_ref[here, :] = jnp.dot(part, rows, preferred_element_type=F32).astype(BF16)
        copies.append(pltpu.make_async_copy(piece_ref.at[here], out_ref.at[here], sems.at[i]))
        copies[-1].start()
    for copy in copies:
        copy.wait()


def expert_kernel(x_hbm, g0, u0, g1, u1, d0, d1, out_hbm, x_ref, wide, tall, out_ref, sems, out_sems):
    ends = [(x_hbm, x_ref)]
    ends += [(w, wide.at[i]) for i, w in enumerate((g0, u0, g1, u1))]
    ends += [(w, tall.at[i]) for i, w in enumerate((d0, d1))]
    loads = [pltpu.make_async_copy(a, b, sems.at[i]) for i, (a, b) in enumerate(ends)]
    for load in loads:
        load.start()
    loads[0].wait()
    x = x_ref[...]
    hidden = []
    for i in (0, 2):
        loads[1 + i].wait()
        gate = jnp.dot(x, wide[i], preferred_element_type=F32)
        loads[2 + i].wait()
        up = jnp.dot(x, wide[i + 1], preferred_element_type=F32)
        hidden.append((gate / (1.0 + jnp.exp(-gate)) * up).astype(BF16))
    loads[5].wait()
    loads[6].wait()
    copies = []
    for i in range(out_ref.shape[0] // PIECE):
        here = pl.ds(i * PIECE, PIECE)
        low, high = (h[i * PIECE : (i + 1) * PIECE, :] for h in hidden)
        total = jnp.dot(low, tall[0], preferred_element_type=F32)
        total = total + jnp.dot(high, tall[1], preferred_element_type=F32)
        out_ref[here, :] = total.astype(BF16)
        copies.append(pltpu.make_async_copy(out_ref.at[here], out_hbm.at[here], out_sems.at[i]))
        copies[-1].start()
    for copy in copies:
        copy.wait()


def weights_kernel(slots, planes, z_ref, extra_ref, high_ref, low_ref):
    tokens, columns = high_ref.shape
    groups = columns // slots
    extra = extra_ref[...].astype(F32)
    gates = extra[:, 8:16] * 256.0 + extra[:, 16:24]
    mix = gates / jnp.sum(gates, axis=1, keepdims=True)
    dest = planes * lax.broadcasted_iota(jnp.int32, (1, EXTRA), 1) + z_ref[0]
    dest = dest.astype(F32)
    match = jnp.zeros((tokens, EXTRA), F32)
    weight = jnp.zeros((tokens, EXTRA), F32)
    for k in range(8):
        same = extra[:, k : k + 1] == dest
        match = match + same.astype(F32)
        weight = weight + jnp.where(same, mix[:, k : k + 1], 0.0)
    lower = lax.broadcasted_iota(jnp.int32, (tokens, tokens), 1) <= lax.broadcasted_iota(
        jnp.int32, (tokens, tokens), 0
    )
    lower = lower.astype(F32).astype(BF16)
    order = jnp.dot(lower, match.astype(BF16), preferred_element_type=F32) * match
    column = lax.broadcasted_iota(jnp.int32, (1, groups * slots), 1)
    group, place = slot_of(column, slots)
    spread = (group == lax.broadcasted_iota(jnp.int32, (EXTRA, 1), 0)).astype(F32).astype(BF16)
    wanted = jnp.dot(order.astype(BF16), spread, preferred_element_type=F32)
    here = wanted == (place + 1).astype(F32)
    high = weight.astype(BF16)
    low = (weight - high.astype(F32)).astype(BF16)
    for piece, ref in ((high, high_ref), (low, low_ref)):
        wide = jnp.dot(piece, spread, preferred_element_type=F32)
        ref[...] = jnp.where(here, wide, 0.0).astype(BF16)


def combine_kernel(home_ref, high_ref, low_ref, *outs):
    home = home_ref[...]
    total = jnp.dot(high_ref[...], home, preferred_element_type=F32)
    total = total + jnp.dot(low_ref[...], home, preferred_element_type=F32)
    start = 0
    for out in outs:
        rows = out.shape[0]
        out[...] = total[start : start + rows, :].astype(out.dtype)
        start += rows


def per_device(tokens, expert_ids, gate_fixed, w_gate, w_up, w_down):
    col_count = lax.axis_size("expert")
    dp_count = lax.axis_size("dp")
    planes = col_count // 2
    half = planes // 2
    width = tokens.shape[1]
    rows = tokens.shape[0] // 2
    chunk = planes * rows
    slots = 3 * chunk // 32
    sent = dp_count * slots
    plane = (lax.axis_index("expert") // 2).astype(jnp.int32).reshape(1)

    def along_z(x, by):
        return lax.ppermute(
            x, "expert", [(i, (i + 2 * by) % col_count) for i in range(col_count)]
        )

    def partner(x):
        return lax.ppermute(x, "expert", [(i, i ^ 1) for i in range(col_count)])

    def exchange(x):
        return lax.all_to_all(x, "dp", split_axis=0, concat_axis=0, tiled=True)

    pieces = sent // PIECE
    moved = ((sent, width), BF16)

    def dispatch(shards):
        return kernel_call(
            functools.partial(dispatch_kernel, slots, planes),
            "dispatch",
            [moved, ((chunk, EXTRA), BF16)],
            [on_chip(x) for x in shards],
            [plane],
            keep=[pltpu.HBM],
            out_specs=[HBM, VMEM],
            scratch=[pltpu.VMEM(*moved), pltpu.SemaphoreType.DMA((pieces,))],
        )

    def mixing(extra):
        return kernel_call(
            functools.partial(weights_kernel, slots, planes),
            "mixing",
            [((chunk, sent), BF16)] * 2,
            [extra],
            [plane],
        )

    panels = []
    for w in (w_gate[0], w_up[0], w_down[0]):
        panels += [w, partner(w)]
    g0, g1, u0, u1, d0, d1 = panels

    def expert(x):
        return kernel_call(
            expert_kernel,
            "expert",
            [moved],
            [off_chip(w) for w in (x, g0, u0, g1, u1, d0, d1)],
            keep=[pltpu.HBM],
            specs=[HBM] * 7,
            out_specs=[HBM],
            scratch=[
                pltpu.VMEM(*moved),
                pltpu.VMEM((4,) + g0.shape, BF16),
                pltpu.VMEM((2,) + d0.shape, BF16),
                pltpu.VMEM(*moved),
                pltpu.SemaphoreType.DMA((7,)),
                pltpu.SemaphoreType.DMA((pieces,)),
            ],
        )[0]

    def combine(home, mix, kinds):
        outs = [((rows, width), kind) for kind in kinds]
        return kernel_call(combine_kernel, "combine", outs, [home] + list(mix), keep=[pltpu.VMEM] * 8)

    def plus(x, part):
        return (x.astype(F32) + part).astype(BF16)

    a, b = kernel_call(
        pack_kernel,
        "pack",
        [((rows, width + EXTRA), BF16)] * 2,
        [off_chip(x) for x in (tokens, expert_ids.T, gate_fixed.T)],
        keep=[pltpu.VMEM] * 2,
    )
    a_up, a_down, b_up, b_down = [a], [a], [b], [b]
    for step in range(1, half):
        for ring, by in ((a_up, 1), (a_down, -1), (b_up, 1), (b_down, -1)):
            ring.append(along_z(ring[-1], by))
    a_up.append(along_z(a_up[-1], 1))
    b_down.append(along_z(b_down[-1], -1))

    near_rows, near_extra = dispatch(
        [a, b, a_up[1], a_down[1], b_up[1], b_down[1], a_up[2], a_down[2]]
    )
    near = off_chip(exchange(near_rows))
    far_rows, far_extra = dispatch(
        [b_up[2], b_down[2], a_up[3], a_down[3], b_up[3], b_down[3], a_up[4], b_down[4]]
    )
    near = after(near, far_rows)
    far = exchange(far_rows)
    near_out = after(expert(near), far)
    near_mix, far_mix = mixing(near_extra), mixing(far_extra)
    far_out = after(expert(far), near_out, *near_mix, *far_mix)
    far_home = exchange(far_out)
    near_home = exchange(after(near_out, far_out))

    kinds = [F32, F32, F32, BF16, BF16, F32, BF16, BF16]
    b_up_2, b_down_2, a_up_3, a_down_3, b_up_3, b_down_3, a_up_4, b_down_4 = combine(
        far_home, far_mix, kinds
    )
    a_low, b_high = along_z(a_up_4, -1), along_z(b_down_4, 1)
    a_high, b_low = along_z(a_down_3, 1), along_z(b_up_3, -1)
    a_low, b_high = along_z(plus(a_low, a_up_3), -1), along_z(plus(b_high, b_down_3), 1)
    near_home = after(near_home, a_low, a_high, b_low)
    b_low, b_high = along_z(plus(b_low, b_up_2), -1), along_z(plus(b_high, b_down_2), 1)
    a_own, b_own, a_up_1, a_down_1, b_up_1, b_down_1, a_up_2, a_down_2 = combine(
        near_home, near_mix, [F32] * 8
    )
    a_low, a_high = along_z(plus(a_low, a_up_2), -1), along_z(plus(a_high, a_down_2), 1)
    b_low, b_high = along_z(plus(b_low, b_up_1), -1), along_z(plus(b_high, b_down_1), 1)
    a_low, a_high = along_z(plus(a_low, a_up_1), -1), along_z(plus(a_high, a_down_1), 1)
    first = a_own + a_low.astype(F32) + a_high.astype(F32)
    second = b_own + b_low.astype(F32) + b_high.astype(F32)
    return jnp.concatenate([first, second], axis=0)


def solution(mesh):
    rows = P(("dp", "expert"), None)
    panels = P(("dp", "expert"), None, None)
    return jax.shard_map(
        per_device,
        mesh=mesh,
        in_specs=(rows, rows, rows, panels, panels, panels),
        out_specs=rows,
        check_vma=False,
    )
```

```python
import functools

import jax
import jax.numpy as jnp
from jax import lax
from jax.experimental import pallas as pl
from jax.experimental.pallas import tpu as pltpu
from jax.sharding import PartitionSpec as P

F32 = jnp.float32
BF16 = jnp.bfloat16
EXTRA = 128
VMEM = pl.BlockSpec(memory_space=pltpu.VMEM)
SMEM = pl.BlockSpec(memory_space=pltpu.SMEM)
HBM = pl.BlockSpec(memory_space=pltpu.HBM)
PIECE = 128
PARAMS = pltpu.CompilerParams(vmem_limit_bytes=24 << 20)


def on_chip(x):
    return pltpu.with_memory_space_constraint(x, pltpu.VMEM)


def off_chip(x):
    return pltpu.with_memory_space_constraint(x, pltpu.HBM)


def after(x, *others):
    return lax.optimization_barrier((x,) + others)[0]


def kernel_call(
    body, name, outs, arrays, scalars=(), keep=(), specs=None, out_specs=None, scratch=()
):
    keep = list(keep) + [jax.ShapeDtypeStruct] * (len(outs) - len(keep))
    return pl.pallas_call(
        body,
        out_shape=[where(*out) for where, out in zip(keep, outs)],
        in_specs=[SMEM] * len(scalars) + (specs or [VMEM] * len(arrays)),
        out_specs=out_specs or [VMEM] * len(outs),
        scratch_shapes=list(scratch),
        compiler_params=PARAMS,
        name=name,
    )(*scalars, *arrays)


def slot_of(index, slots):
    group = jnp.zeros_like(index)
    for d in range(1, 16):
        group = group + (index >= d * slots).astype(jnp.int32)
    return group, index - group * slots


def pack_kernel(tokens_ref, ids_ref, gates_ref, out_ref):
    rows, width = tokens_ref.shape
    gates = gates_ref[...]
    columns = [ids_ref[...], gates >> 8, gates & 255]
    top = jnp.concatenate(columns, axis=0).astype(F32)
    top = jnp.concatenate([top, jnp.zeros((top.shape[0], EXTRA - rows), F32)], axis=1)
    extra = jnp.concatenate([top, jnp.zeros((EXTRA - top.shape[0], EXTRA), F32)], axis=0).T
    out_ref[:, :width] = tokens_ref[...]
    out_ref[:, width:] = extra[:rows, :].astype(BF16)


def dispatch_kernel(slots, planes, z_ref, *refs):
    refs, (out_ref, extra_ref, piece_ref, sems) = refs[:-4], refs[-4:]
    width = out_ref.shape[1]
    groups = out_ref.shape[0] // slots
    extra = jnp.concatenate([x[:, width:] for x in refs], axis=0)
    extra_ref[...] = extra
    extra = extra.astype(F32).T
    tokens = extra.shape[1]
    dest = planes * lax.broadcasted_iota(jnp.int32, (groups, 1), 0) + z_ref[0]
    dest = dest.astype(F32)
    match = jnp.zeros((groups, tokens), F32)
    for k in range(8):
        match = match + (extra[k : k + 1, :] == dest).astype(F32)
    upper = lax.broadcasted_iota(jnp.int32, (tokens, tokens), 0) <= lax.broadcasted_iota(
        jnp.int32, (tokens, tokens), 1
    )
    upper = upper.astype(F32).astype(BF16)
    order = jnp.dot(match.astype(BF16), upper, preferred_element_type=F32) * match
    row = lax.broadcasted_iota(jnp.int32, (groups * slots, 1), 0)
    group, place = slot_of(row, slots)
    spread = (group == lax.broadcasted_iota(jnp.int32, (1, groups), 1)).astype(F32).astype(BF16)
    wanted = jnp.dot(spread, order.astype(BF16), preferred_element_type=F32)
    pick = (wanted == (place + 1).astype(F32)).astype(F32).astype(BF16)
    rows = jnp.concatenate([x[:, :width] for x in refs], axis=0)
    copies = []
    for i in range(out_ref.shape[0] // PIECE):
        here = pl.ds(i * PIECE, PIECE)
        part = pick[i * PIECE : (i + 1) * PIECE, :]
        piece_ref[here, :] = jnp.dot(part, rows, preferred_element_type=F32).astype(BF16)
        copies.append(pltpu.make_async_copy(piece_ref.at[here], out_ref.at[here], sems.at[i]))
        copies[-1].start()
    for copy in copies:
        copy.wait()


def expert_kernel(x_hbm, g0, u0, g1, u1, d0, d1, out_hbm, x_ref, wide, tall, out_ref, sems, out_sems):
    units = g0.shape[1]
    ends = [(x_hbm, x_ref)]
    ends += [(w, wide.at[:, pl.ds(i * units, units)]) for i, w in enumerate((g0, u0, g1, u1))]
    ends += [(w, tall.at[pl.ds(i * units, units)]) for i, w in enumerate((d0, d1))]
    loads = [pltpu.make_async_copy(a, b, sems.at[i]) for i, (a, b) in enumerate(ends)]
    for load in loads:
        load.start()
    loads[0].wait()
    x = x_ref[...]
    hidden = []
    for i in (0, 2):
        loads[1 + i].wait()
        loads[2 + i].wait()
        both = jnp.dot(
            x, wide[:, i * units : (i + 2) * units], preferred_element_type=F32
        )
        gate, up = both[:, :units], both[:, units:]
        hidden.append((gate / (1.0 + jnp.exp(-gate)) * up).astype(BF16))
    hidden = jnp.concatenate(hidden, axis=1)
    loads[5].wait()
    loads[6].wait()
    copies = []
    for i in range(out_ref.shape[0] // PIECE):
        here = pl.ds(i * PIECE, PIECE)
        total = jnp.dot(
            hidden[i * PIECE : (i + 1) * PIECE, :], tall[...], preferred_element_type=F32
        )
        out_ref[here, :] = total.astype(BF16)
        copies.append(pltpu.make_async_copy(out_ref.at[here], out_hbm.at[here], out_sems.at[i]))
        copies[-1].start()
    for copy in copies:
        copy.wait()


def weights_kernel(slots, planes, z_ref, extra_ref, high_ref, low_ref):
    tokens, columns = high_ref.shape
    groups = columns // slots
    extra = extra_ref[...].astype(F32)
    gates = extra[:, 8:16] * 256.0 + extra[:, 16:24]
    mix = gates / jnp.sum(gates, axis=1, keepdims=True)
    dest = planes * lax.broadcasted_iota(jnp.int32, (1, EXTRA), 1) + z_ref[0]
    dest = dest.astype(F32)
    match = jnp.zeros((tokens, EXTRA), F32)
    weight = jnp.zeros((tokens, EXTRA), F32)
    for k in range(8):
        same = extra[:, k : k + 1] == dest
        match = match + same.astype(F32)
        weight = weight + jnp.where(same, mix[:, k : k + 1], 0.0)
    lower = lax.broadcasted_iota(jnp.int32, (tokens, tokens), 1) <= lax.broadcasted_iota(
        jnp.int32, (tokens, tokens), 0
    )
    lower = lower.astype(F32).astype(BF16)
    order = jnp.dot(lower, match.astype(BF16), preferred_element_type=F32) * match
    column = lax.broadcasted_iota(jnp.int32, (1, groups * slots), 1)
    group, place = slot_of(column, slots)
    spread = (group == lax.broadcasted_iota(jnp.int32, (EXTRA, 1), 0)).astype(F32).astype(BF16)
    wanted = jnp.dot(order.astype(BF16), spread, preferred_element_type=F32)
    here = wanted == (place + 1).astype(F32)
    high = weight.astype(BF16)
    low = (weight - high.astype(F32)).astype(BF16)
    for piece, ref in ((high, high_ref), (low, low_ref)):
        wide = jnp.dot(piece, spread, preferred_element_type=F32)
        ref[...] = jnp.where(here, wide, 0.0).astype(BF16)


def combine_kernel(home_ref, high_ref, low_ref, *outs):
    home = home_ref[...]
    total = jnp.dot(high_ref[...], home, preferred_element_type=F32)
    total = total + jnp.dot(low_ref[...], home, preferred_element_type=F32)
    start = 0
    for out in outs:
        rows = out.shape[0]
        out[...] = total[start : start + rows, :].astype(out.dtype)
        start += rows


def per_device(tokens, expert_ids, gate_fixed, w_gate, w_up, w_down):
    col_count = lax.axis_size("expert")
    dp_count = lax.axis_size("dp")
    planes = col_count // 2
    half = planes // 2
    rows, width = tokens.shape
    chunk = half * rows
    slots = 3 * chunk // 32
    sent = dp_count * slots
    plane = (lax.axis_index("expert") // 2).astype(jnp.int32).reshape(1)

    def along_z(x, by):
        return lax.ppermute(
            x, "expert", [(i, (i + 2 * by) % col_count) for i in range(col_count)]
        )

    def partner(x):
        return lax.ppermute(x, "expert", [(i, i ^ 1) for i in range(col_count)])

    def exchange(x):
        return lax.all_to_all(x, "dp", split_axis=0, concat_axis=0, tiled=True)

    pieces = sent // PIECE
    moved = ((sent, width), BF16)

    def dispatch(shards):
        return kernel_call(
            functools.partial(dispatch_kernel, slots, planes),
            "dispatch",
            [moved, ((chunk, EXTRA), BF16)],
            [on_chip(x) for x in shards],
            [plane],
            keep=[pltpu.HBM],
            out_specs=[HBM, VMEM],
            scratch=[pltpu.VMEM(*moved), pltpu.SemaphoreType.DMA((pieces,))],
        )

    def mixing(extra):
        return kernel_call(
            functools.partial(weights_kernel, slots, planes),
            "mixing",
            [((chunk, sent), BF16)] * 2,
            [extra],
            [plane],
        )

    panels = []
    for w in (w_gate[0], w_up[0], w_down[0]):
        panels += [w, partner(w)]
    g0, g1, u0, u1, d0, d1 = panels

    def expert(x):
        return kernel_call(
            expert_kernel,
            "expert",
            [moved],
            [off_chip(w) for w in (x, g0, u0, g1, u1, d0, d1)],
            keep=[pltpu.HBM],
            specs=[HBM] * 7,
            out_specs=[HBM],
            scratch=[
                pltpu.VMEM(*moved),
                pltpu.VMEM((g0.shape[0], 4 * g0.shape[1]), BF16),
                pltpu.VMEM((2 * d0.shape[0], d0.shape[1]), BF16),
                pltpu.VMEM(*moved),
                pltpu.SemaphoreType.DMA((7,)),
                pltpu.SemaphoreType.DMA((pieces,)),
            ],
        )[0]

    def combine(home, mix, kinds):
        outs = [((rows, width), kind) for kind in kinds]
        return kernel_call(combine_kernel, "combine", outs, [home] + list(mix), keep=[pltpu.VMEM] * 4)

    def plus(x, part):
        return (x.astype(F32) + part).astype(BF16)

    mine = kernel_call(
        pack_kernel,
        "pack",
        [((rows, width + EXTRA), BF16)],
        [off_chip(x) for x in (tokens, expert_ids.T, gate_fixed.T)],
        keep=[pltpu.VMEM],
    )[0]
    low_1, high_1 = along_z(mine, 1), along_z(mine, -1)
    low_2, high_2 = along_z(low_1, 1), along_z(high_1, -1)
    low_3, high_3 = along_z(low_2, 1), along_z(high_2, -1)
    low_4 = along_z(low_3, 1)

    near_rows, near_extra = dispatch([mine, low_1, high_1, low_2])
    near = off_chip(exchange(after(near_rows, high_2)))
    far_rows, far_extra = dispatch([high_2, low_3, high_3, low_4])
    near = after(near, far_rows)
    far = exchange(far_rows)
    near_out = after(expert(near), far)
    near_mix, far_mix = mixing(near_extra), mixing(far_extra)
    far_out = after(expert(far), near_out, *near_mix, *far_mix)
    far_home = exchange(far_out)
    near_home = exchange(after(near_out, far_home))
    to_high_2, to_low_3, to_high_3, to_low_4 = combine(far_home, far_mix, [F32, F32, BF16, BF16])
    down, up = along_z(to_low_4, -1), along_z(to_high_3, 1)
    down, up = along_z(plus(down, to_low_3), -1), along_z(plus(up, to_high_2), 1)
    near_home = after(near_home, down, up)
    own, to_low_1, to_high_1, to_low_2 = combine(near_home, near_mix, [F32] * 4)
    down, up = along_z(plus(down, to_low_2), -1), along_z(plus(up, to_high_1), 1)
    down = along_z(plus(down, to_low_1), -1)
    return own + up.astype(F32) + down.astype(F32)


def solution(mesh):
    rows = P(("dp", "expert"), None)
    panels = P(("dp", "expert"), None, None)
    return jax.shard_map(
        per_device,
        mesh=mesh,
        in_specs=(rows, rows, rows, panels, panels, panels),
        out_specs=rows,
        check_vma=False,
    )
```

```python
import functools

import jax
import jax.numpy as jnp
from jax import lax
from jax.experimental import pallas as pl
from jax.experimental.pallas import tpu as pltpu
from jax.sharding import PartitionSpec as P

F32 = jnp.float32
BF16 = jnp.bfloat16
EXTRA = 128
VMEM = pl.BlockSpec(memory_space=pltpu.VMEM)
SMEM = pl.BlockSpec(memory_space=pltpu.SMEM)
HBM = pl.BlockSpec(memory_space=pltpu.HBM)
LANES = 512
PARAMS = pltpu.CompilerParams(vmem_limit_bytes=24 << 20)


def on_chip(x):
    return pltpu.with_memory_space_constraint(x, pltpu.VMEM)


def off_chip(x):
    return pltpu.with_memory_space_constraint(x, pltpu.HBM)


def after(x, *others):
    return lax.optimization_barrier((x,) + others)[0]


def kernel_call(
    body, name, outs, arrays, scalars=(), keep=(), specs=None, out_specs=None, scratch=()
):
    keep = list(keep) + [jax.ShapeDtypeStruct] * (len(outs) - len(keep))
    return pl.pallas_call(
        body,
        out_shape=[where(*out) for where, out in zip(keep, outs)],
        in_specs=[SMEM] * len(scalars) + (specs or [VMEM] * len(arrays)),
        out_specs=out_specs or [VMEM] * len(outs),
        scratch_shapes=list(scratch),
        compiler_params=PARAMS,
        name=name,
    )(*scalars, *arrays)


def slot_of(index, slots):
    group = jnp.zeros_like(index)
    for d in range(1, 16):
        group = group + (index >= d * slots).astype(jnp.int32)
    return group, index - group * slots


def pack_kernel(tokens_ref, ids_ref, gates_ref, out_ref):
    rows, width = tokens_ref.shape
    gates = gates_ref[...]
    columns = [ids_ref[...], gates >> 8, gates & 255]
    top = jnp.concatenate(columns, axis=0).astype(F32)
    top = jnp.concatenate([top, jnp.zeros((top.shape[0], EXTRA - rows), F32)], axis=1)
    extra = jnp.concatenate([top, jnp.zeros((EXTRA - top.shape[0], EXTRA), F32)], axis=0).T
    out_ref[:, :width] = tokens_ref[...]
    out_ref[:, width:] = extra[:rows, :].astype(BF16)


def to_blocks(rows_ref, blocks_ref, base, slots, groups, total=None, offset=0):
    parts = rows_ref.shape[1] // LANES
    for d in groups:
        rows = rows_ref[pl.ds(base + d * slots, slots), :]
        for q in range(parts):
            there = pl.ds((d * parts + q) * (total or slots) + offset, slots)
            blocks_ref[there, :] = rows[:, q * LANES : (q + 1) * LANES]


def to_rows(blocks_ref, rows_ref, base, slots, groups, total=None, offset=0):
    parts = rows_ref.shape[1] // LANES
    for d in groups:
        for q in range(parts):
            here = pl.ds((d * parts + q) * (total or slots) + offset, slots)
            there = pl.ds(base + d * slots, slots)
            rows_ref[there, q * LANES : (q + 1) * LANES] = blocks_ref[here, :]


def pick_rows(extra, planes, groups, slots, plane):
    tokens = extra.shape[0]
    extra = extra.astype(F32)
    spare = -tokens % EXTRA
    if spare:
        extra = jnp.concatenate([extra, jnp.zeros((spare, EXTRA), F32)], axis=0)
    extra = extra.T[:8, :tokens]
    dest = planes * lax.broadcasted_iota(jnp.int32, (groups, 1), 0) + plane
    dest = dest.astype(F32)
    match = jnp.zeros((groups, tokens), F32)
    for k in range(8):
        match = match + (extra[k : k + 1, :] == dest).astype(F32)
    upper = lax.broadcasted_iota(jnp.int32, (tokens, tokens), 0) <= lax.broadcasted_iota(
        jnp.int32, (tokens, tokens), 1
    )
    upper = upper.astype(F32).astype(BF16)
    order = jnp.dot(match.astype(BF16), upper, preferred_element_type=F32) * match
    row = lax.broadcasted_iota(jnp.int32, (groups * slots, 1), 0)
    group, place = slot_of(row, slots)
    spread = (group == lax.broadcasted_iota(jnp.int32, (1, groups), 1)).astype(F32).astype(BF16)
    wanted = jnp.dot(spread, order.astype(BF16), preferred_element_type=F32)
    return (wanted == (place + 1).astype(F32)).astype(F32).astype(BF16)


def dispatch_kernel(sizes, slots, planes, groups, z_ref, *refs):
    count = sum(sizes)
    shards, refs = refs[:count], refs[count:]
    out_ref, extras, (rows_ref, block_ref, sems) = refs[0], refs[1:-3], refs[-3:]
    width = rows_ref.shape[1]
    base, offset, total = 0, 0, sum(slots)
    for i, (size, take) in enumerate(zip(sizes, slots)):
        mine, shards = shards[:size], shards[size:]
        extra = jnp.concatenate([x[:, width:] for x in mine], axis=0)
        extras[i][...] = extra
        pick = pick_rows(extra, planes, groups, take, z_ref[0])
        rows = jnp.concatenate([x[:, :width] for x in mine], axis=0)
        rows_ref[pl.ds(base, groups * take), :] = jnp.dot(
            pick, rows, preferred_element_type=F32
        ).astype(BF16)
        base += groups * take
    size = block_ref.shape[0] // 2
    copies = []
    for i in range(2):
        half = groups // 2
        base, offset = 0, 0
        for take in slots:
            to_blocks(
                rows_ref, block_ref, base, take, range(i * half, (i + 1) * half), total, offset
            )
            base += groups * take
            offset += take
        here = pl.ds(i * size, size)
        copies.append(pltpu.make_async_copy(block_ref.at[here], out_ref.at[here], sems.at[i]))
        copies[-1].start()
    for copy in copies:
        copy.wait()


def feed_forward(x_ref, wide, tall, out_ref, loads):
    units = tall.shape[0] // 2
    x = x_ref[...]
    hidden = []
    for i in (0, 2):
        for load in loads[i : i + 2]:
            load.wait()
        both = jnp.dot(x, wide[:, i * units : (i + 2) * units], preferred_element_type=F32)
        gate, up = both[:, :units], both[:, units:]
        hidden.append((gate / (1.0 + jnp.exp(-gate)) * up).astype(BF16))
    hidden = jnp.concatenate(hidden, axis=1)
    for load in loads[4:]:
        load.wait()
    out_ref[...] = jnp.dot(hidden, tall[...], preferred_element_type=F32).astype(BF16)


def weight_loads(panels, wide, tall, sems):
    units = panels[0].shape[1]
    ends = [(w, wide.at[:, pl.ds(i * units, units)]) for i, w in enumerate(panels[:4])]
    ends += [(w, tall.at[pl.ds(i * units, units)]) for i, w in enumerate(panels[4:])]
    return [pltpu.make_async_copy(a, b, sems.at[i]) for i, (a, b) in enumerate(ends)]


def expert_kernel(slots, groups, *refs):
    count = len(slots)
    flat = [take for part in slots for take in part]
    chunks, panels, refs = refs[:count], refs[count : count + 6], refs[count + 6 :]
    outs, refs = refs[: len(flat)], refs[len(flat) :]
    wide, tall, x_ref, out_ref = refs[:4]
    blocks, refs = refs[4 : 4 + count], refs[4 + count :]
    leaving, (sems, chunk_sems, out_sems) = refs[: len(flat)], refs[len(flat) :]
    arrive = [pltpu.make_async_copy(chunks[i], blocks[i], chunk_sems.at[i]) for i in range(count)]
    loads = weight_loads(panels, wide, tall, sems)
    for copy in arrive + loads:
        copy.start()
    base = 0
    for i in range(count):
        arrive[i].wait()
        offset = 0
        for take in slots[i]:
            to_rows(blocks[i], x_ref, base, take, range(groups), sum(slots[i]), offset)
            base += groups * take
            offset += take
    feed_forward(x_ref, wide, tall, out_ref, loads)
    leave, base = [], 0
    for i, take in enumerate(flat):
        to_blocks(out_ref, leaving[i], base, take, range(groups))
        base += groups * take
        leave.append(pltpu.make_async_copy(leaving[i], outs[i], out_sems.at[i]))
        leave[-1].start()
    for copy in leave:
        copy.wait()


def last_kernel(slots, groups, chunk_ref, g0, u0, g1, u1, d0, d1, out_hbm, *refs):
    wide, tall, x_ref, out_ref, block_ref, sems, out_sems = refs
    loads = weight_loads((g0, u0, g1, u1, d0, d1), wide, tall, sems)
    for load in loads:
        load.start()
    to_rows(chunk_ref, x_ref, 0, slots, range(groups))
    feed_forward(x_ref, wide, tall, out_ref, loads)
    size = block_ref.shape[0] // 2
    copies = []
    for i in range(2):
        half = groups // 2
        to_blocks(out_ref, block_ref, 0, slots, range(i * half, (i + 1) * half))
        here = pl.ds(i * size, size)
        copies.append(pltpu.make_async_copy(block_ref.at[here], out_hbm.at[here], out_sems.at[i]))
        copies[-1].start()
    for copy in copies:
        copy.wait()


def mixing_kernel(slots, planes, groups, z_ref, *refs):
    count = len(slots)
    for i in range(count):
        mix_slots(slots[i], planes, groups, z_ref, refs[i], *refs[count + 2 * i : count + 2 * i + 2])


def mix_slots(slots, planes, groups, z_ref, extra_ref, high_ref, low_ref):
    tokens = extra_ref.shape[0]
    extra = extra_ref[...].astype(F32)
    gates = extra[:, 8:16] * 256.0 + extra[:, 16:24]
    mix = gates / jnp.sum(gates, axis=1, keepdims=True)
    dest = planes * lax.broadcasted_iota(jnp.int32, (1, EXTRA), 1) + z_ref[0]
    dest = dest.astype(F32)
    match = jnp.zeros((tokens, EXTRA), F32)
    weight = jnp.zeros((tokens, EXTRA), F32)
    for k in range(8):
        same = extra[:, k : k + 1] == dest
        match = match + same.astype(F32)
        weight = weight + jnp.where(same, mix[:, k : k + 1], 0.0)
    lower = lax.broadcasted_iota(jnp.int32, (tokens, tokens), 1) <= lax.broadcasted_iota(
        jnp.int32, (tokens, tokens), 0
    )
    lower = lower.astype(F32).astype(BF16)
    order = jnp.dot(lower, match.astype(BF16), preferred_element_type=F32) * match
    column = lax.broadcasted_iota(jnp.int32, (1, groups * slots), 1)
    group, place = slot_of(column, slots)
    spread = (group == lax.broadcasted_iota(jnp.int32, (EXTRA, 1), 0)).astype(F32).astype(BF16)
    wanted = jnp.dot(order.astype(BF16), spread, preferred_element_type=F32)
    here = wanted == (place + 1).astype(F32)
    high = weight.astype(BF16)
    low = (weight - high.astype(F32)).astype(BF16)
    for piece, ref in ((high, high_ref), (low, low_ref)):
        wide = jnp.dot(piece, spread, preferred_element_type=F32)
        ref[...] = jnp.where(here, wide, 0.0).astype(BF16)


def combine_kernel(slots, groups, home_ref, high_ref, low_ref, *outs):
    outs, rows_ref = outs[:-1], outs[-1]
    to_rows(home_ref, rows_ref, 0, slots, range(groups))
    home = rows_ref[...]
    total = jnp.dot(high_ref[...], home, preferred_element_type=F32)
    total = total + jnp.dot(low_ref[...], home, preferred_element_type=F32)
    start = 0
    for out in outs:
        rows = out.shape[0]
        out[...] = total[start : start + rows, :].astype(out.dtype)
        start += rows


def per_device(tokens, expert_ids, gate_fixed, w_gate, w_up, w_down):
    col_count = lax.axis_size("expert")
    groups = lax.axis_size("dp")
    planes = col_count // 2
    rows, width = tokens.shape
    units = w_gate.shape[2]
    parts = width // LANES
    per_shard = 3 * rows // 32
    plane = (lax.axis_index("expert") // 2).astype(jnp.int32).reshape(1)

    def along_z(x, by):
        return lax.ppermute(
            x, "expert", [(i, (i + 2 * by) % col_count) for i in range(col_count)]
        )

    def partner(x):
        return lax.ppermute(x, "expert", [(i, i ^ 1) for i in range(col_count)])

    def exchange(x):
        return lax.all_to_all(x, "dp", split_axis=0, concat_axis=0, tiled=True)

    def full(slots):
        return ((groups * slots, width), BF16)

    def packed(slots):
        return ((groups * slots * parts, LANES), BF16)

    def dispatch(*sets):
        sizes = [len(shards) for shards in sets]
        slots = [per_shard * size for size in sizes]
        total = sum(slots)
        return kernel_call(
            functools.partial(dispatch_kernel, sizes, slots, planes, groups),
            "dispatch",
            [packed(total)] + [((rows * size, EXTRA), BF16) for size in sizes],
            [on_chip(x) for shards in sets for x in shards],
            [plane],
            keep=[pltpu.HBM],
            out_specs=[HBM] + [VMEM] * len(sizes),
            scratch=[
                pltpu.VMEM(*full(total)),
                pltpu.VMEM(*packed(total)),
                pltpu.SemaphoreType.DMA((2,)),
            ],
        )

    def mixing(extras):
        slots = [per_shard * x.shape[0] // rows for x in extras]
        shapes = [((x.shape[0], groups * n), BF16) for x, n in zip(extras, slots)]
        mixes = kernel_call(
            functools.partial(mixing_kernel, slots, planes, groups),
            "mixing",
            [shape for shape in shapes for _ in range(2)],
            extras,
            [plane],
        )
        return list(zip(mixes[::2], mixes[1::2]))

    panels = []
    for w in (w_gate[0], w_up[0], w_down[0]):
        panels += [w, partner(w)]
    g0, g1, u0, u1, d0, d1 = panels
    wide, tall = ((width, 4 * units), BF16), ((2 * units, width), BF16)

    def expert(chunks, slots):
        count = len(chunks)
        flat = [take for part in slots for take in part]
        return kernel_call(
            functools.partial(expert_kernel, slots, groups),
            "expert",
            [packed(n) for n in flat],
            [off_chip(w) for w in (*chunks, g0, u0, g1, u1, d0, d1)],
            keep=[pltpu.HBM] * len(flat),
            specs=[HBM] * (count + 6),
            out_specs=[HBM] * len(flat),
            scratch=[
                pltpu.VMEM(*wide),
                pltpu.VMEM(*tall),
                pltpu.VMEM(*full(sum(flat))),
                pltpu.VMEM(*full(sum(flat))),
                *[pltpu.VMEM(*packed(sum(part))) for part in slots],
                *[pltpu.VMEM(*packed(n)) for n in flat],
                pltpu.SemaphoreType.DMA((6,)),
                pltpu.SemaphoreType.DMA((count,)),
                pltpu.SemaphoreType.DMA((len(flat),)),
            ],
        )

    def last(chunk, slots):
        return kernel_call(
            functools.partial(last_kernel, slots, groups),
            "last",
            [packed(slots)],
            [chunk] + [off_chip(w) for w in (g0, u0, g1, u1, d0, d1)],
            keep=[pltpu.HBM],
            specs=[VMEM] + [HBM] * 6,
            out_specs=[HBM],
            scratch=[
                pltpu.VMEM(*wide),
                pltpu.VMEM(*tall),
                pltpu.VMEM(*full(slots)),
                pltpu.VMEM(*full(slots)),
                pltpu.VMEM(*packed(slots)),
                pltpu.SemaphoreType.DMA((6,)),
                pltpu.SemaphoreType.DMA((2,)),
            ],
        )[0]

    def combine(home, mix, kinds):
        slots = per_shard * len(kinds)
        return kernel_call(
            functools.partial(combine_kernel, slots, groups),
            "combine",
            [((rows, width), kind) for kind in kinds],
            [home] + list(mix),
            keep=[pltpu.VMEM] * len(kinds),
            scratch=[pltpu.VMEM(*full(slots))],
        )

    def plus(x, part):
        return (x.astype(F32) + part).astype(BF16)

    mine = kernel_call(
        pack_kernel,
        "pack",
        [((rows, width + EXTRA), BF16)],
        [off_chip(x) for x in (tokens, expert_ids.T, gate_fixed.T)],
        keep=[pltpu.VMEM],
    )[0]
    low_1, high_1 = along_z(mine, 1), along_z(mine, -1)
    low_2, high_2 = along_z(low_1, 1), along_z(high_1, -1)
    low_3, high_3 = along_z(low_2, 1), along_z(high_2, -1)
    low_4 = along_z(low_3, 1)

    near_rows, extra_0, extra_1 = dispatch([mine], [low_1, high_1])
    near = off_chip(exchange(near_rows))
    rows_2, extra_2 = dispatch([low_2, high_2])
    there_2 = off_chip(exchange(after(rows_2, near, low_3, high_3)))
    rows_3, extra_3 = dispatch([low_3, high_3, low_4])
    there_3 = exchange(after(rows_3, there_2))
    first = [after(x, rows_3) for x in (near, there_2)]
    one, two, three = per_shard, 2 * per_shard, 3 * per_shard
    out_0, out_1, out_2 = expert(first, [[one, two], [two]])
    mix_0, mix_1, mix_2, mix_3 = mixing([extra_0, extra_1, extra_2, extra_3])
    there_3 = after(there_3, out_0, *mix_0)
    out_3 = last(there_3, three)

    back_3 = exchange(out_3)
    back_2 = exchange(after(out_2, back_3))
    back_1 = exchange(after(out_1, back_2))
    back_0 = exchange(after(out_0, back_1))
    to_low_3, to_high_3, to_low_4 = combine(back_3, mix_3, [F32, BF16, BF16])
    down, up = along_z(to_low_4, -1), along_z(to_high_3, 1)
    back_2 = after(back_2, down, up)
    down = along_z(plus(down, to_low_3), -1)
    to_low_2, to_high_2 = combine(back_2, mix_2, [F32] * 2)
    up = along_z(plus(up, to_high_2), 1)
    back_1 = after(back_1, down, up)
    down = along_z(plus(down, to_low_2), -1)
    to_low_1, to_high_1 = combine(back_1, mix_1, [F32] * 2)
    down, up = along_z(plus(down, to_low_1), -1), along_z(plus(up, to_high_1), 1)
    (own,) = combine(back_0, mix_0, [F32])
    return own + up.astype(F32) + down.astype(F32)


def solution(mesh):
    rows = P(("dp", "expert"), None)
    panels = P(("dp", "expert"), None, None)
    return jax.shard_map(
        per_device,
        mesh=mesh,
        in_specs=(rows, rows, rows, panels, panels, panels),
        out_specs=rows,
        check_vma=False,
    )
```

```python
import functools

import jax
import jax.numpy as jnp
from jax import lax
from jax.experimental import pallas as pl
from jax.experimental.pallas import tpu as pltpu
from jax.sharding import PartitionSpec as P

F32 = jnp.float32
BF16 = jnp.bfloat16
EXTRA = 128
VMEM = pl.BlockSpec(memory_space=pltpu.VMEM)
SMEM = pl.BlockSpec(memory_space=pltpu.SMEM)
HBM = pl.BlockSpec(memory_space=pltpu.HBM)
PIECE = 128
PARAMS = pltpu.CompilerParams(vmem_limit_bytes=24 << 20)


def on_chip(x):
    return pltpu.with_memory_space_constraint(x, pltpu.VMEM)


def off_chip(x):
    return pltpu.with_memory_space_constraint(x, pltpu.HBM)


def after(x, *others):
    return lax.optimization_barrier((x,) + others)[0]


def kernel_call(
    body, name, outs, arrays, scalars=(), keep=(), specs=None, out_specs=None, scratch=()
):
    keep = list(keep) + [jax.ShapeDtypeStruct] * (len(outs) - len(keep))
    return pl.pallas_call(
        body,
        out_shape=[where(*out) for where, out in zip(keep, outs)],
        in_specs=[SMEM] * len(scalars) + (specs or [VMEM] * len(arrays)),
        out_specs=out_specs or [VMEM] * len(outs),
        scratch_shapes=list(scratch),
        compiler_params=PARAMS,
        name=name,
    )(*scalars, *arrays)


def slot_of(index, slots):
    group = jnp.zeros_like(index)
    for d in range(1, 16):
        group = group + (index >= d * slots).astype(jnp.int32)
    return group, index - group * slots


def pack_kernel(tokens_ref, ids_ref, gates_ref, out_ref):
    rows, width = tokens_ref.shape
    gates = gates_ref[...]
    columns = [ids_ref[...], gates >> 8, gates & 255]
    top = jnp.concatenate(columns, axis=0).astype(F32)
    top = jnp.concatenate([top, jnp.zeros((top.shape[0], EXTRA - rows), F32)], axis=1)
    extra = jnp.concatenate([top, jnp.zeros((EXTRA - top.shape[0], EXTRA), F32)], axis=0).T
    out_ref[:, :width] = tokens_ref[...]
    out_ref[:, width:] = extra[:rows, :].astype(BF16)


def dispatch_kernel(slots, planes, z_ref, *refs):
    refs, (out_ref, extra_ref, piece_ref, sems) = refs[:-4], refs[-4:]
    width = out_ref.shape[1]
    groups = out_ref.shape[0] // slots
    extra = jnp.concatenate([x[:, width:] for x in refs], axis=0)
    extra_ref[...] = extra
    extra = extra.astype(F32).T
    tokens = extra.shape[1]
    dest = planes * lax.broadcasted_iota(jnp.int32, (groups, 1), 0) + z_ref[0]
    dest = dest.astype(F32)
    match = jnp.zeros((groups, tokens), F32)
    for k in range(8):
        match = match + (extra[k : k + 1, :] == dest).astype(F32)
    upper = lax.broadcasted_iota(jnp.int32, (tokens, tokens), 0) <= lax.broadcasted_iota(
        jnp.int32, (tokens, tokens), 1
    )
    upper = upper.astype(F32).astype(BF16)
    order = jnp.dot(match.astype(BF16), upper, preferred_element_type=F32) * match
    row = lax.broadcasted_iota(jnp.int32, (groups * slots, 1), 0)
    group, place = slot_of(row, slots)
    spread = (group == lax.broadcasted_iota(jnp.int32, (1, groups), 1)).astype(F32).astype(BF16)
    wanted = jnp.dot(spread, order.astype(BF16), preferred_element_type=F32)
    pick = (wanted == (place + 1).astype(F32)).astype(F32).astype(BF16)
    rows = jnp.concatenate([x[:, :width] for x in refs], axis=0)
    copies = []
    for i in range(out_ref.shape[0] // PIECE):
        here = pl.ds(i * PIECE, PIECE)
        part = pick[i * PIECE : (i + 1) * PIECE, :]
        piece_ref[here, :] = jnp.dot(part, rows, preferred_element_type=F32).astype(BF16)
        copies.append(pltpu.make_async_copy(piece_ref.at[here], out_ref.at[here], sems.at[i]))
        copies[-1].start()
    for copy in copies:
        copy.wait()


def expert_kernel(x_ref, g0, u0, g1, u1, d0, d1, out_hbm, wide, tall, out_ref, sems, out_sems):
    units = g0.shape[1]
    ends = [(w, wide.at[:, pl.ds(i * units, units)]) for i, w in enumerate((g0, u0, g1, u1))]
    ends += [(w, tall.at[pl.ds(i * units, units)]) for i, w in enumerate((d0, d1))]
    loads = [pltpu.make_async_copy(a, b, sems.at[i]) for i, (a, b) in enumerate(ends)]
    for load in loads:
        load.start()
    x = x_ref[...]
    hidden = []
    for i in (0, 2):
        loads[i].wait()
        loads[i + 1].wait()
        both = jnp.dot(
            x, wide[:, i * units : (i + 2) * units], preferred_element_type=F32
        )
        gate, up = both[:, :units], both[:, units:]
        hidden.append((gate / (1.0 + jnp.exp(-gate)) * up).astype(BF16))
    hidden = jnp.concatenate(hidden, axis=1)
    loads[4].wait()
    loads[5].wait()
    copies = []
    for i in range(out_ref.shape[0] // PIECE):
        here = pl.ds(i * PIECE, PIECE)
        total = jnp.dot(
            hidden[i * PIECE : (i + 1) * PIECE, :], tall[...], preferred_element_type=F32
        )
        out_ref[here, :] = total.astype(BF16)
        copies.append(pltpu.make_async_copy(out_ref.at[here], out_hbm.at[here], out_sems.at[i]))
        copies[-1].start()
    for copy in copies:
        copy.wait()


def weights_kernel(slots, planes, z_ref, extra_ref, high_ref, low_ref):
    tokens, columns = high_ref.shape
    groups = columns // slots
    extra = extra_ref[...].astype(F32)
    gates = extra[:, 8:16] * 256.0 + extra[:, 16:24]
    mix = gates / jnp.sum(gates, axis=1, keepdims=True)
    dest = planes * lax.broadcasted_iota(jnp.int32, (1, EXTRA), 1) + z_ref[0]
    dest = dest.astype(F32)
    match = jnp.zeros((tokens, EXTRA), F32)
    weight = jnp.zeros((tokens, EXTRA), F32)
    for k in range(8):
        same = extra[:, k : k + 1] == dest
        match = match + same.astype(F32)
        weight = weight + jnp.where(same, mix[:, k : k + 1], 0.0)
    lower = lax.broadcasted_iota(jnp.int32, (tokens, tokens), 1) <= lax.broadcasted_iota(
        jnp.int32, (tokens, tokens), 0
    )
    lower = lower.astype(F32).astype(BF16)
    order = jnp.dot(lower, match.astype(BF16), preferred_element_type=F32) * match
    column = lax.broadcasted_iota(jnp.int32, (1, groups * slots), 1)
    group, place = slot_of(column, slots)
    spread = (group == lax.broadcasted_iota(jnp.int32, (EXTRA, 1), 0)).astype(F32).astype(BF16)
    wanted = jnp.dot(order.astype(BF16), spread, preferred_element_type=F32)
    here = wanted == (place + 1).astype(F32)
    high = weight.astype(BF16)
    low = (weight - high.astype(F32)).astype(BF16)
    for piece, ref in ((high, high_ref), (low, low_ref)):
        wide = jnp.dot(piece, spread, preferred_element_type=F32)
        ref[...] = jnp.where(here, wide, 0.0).astype(BF16)


def combine_kernel(home_ref, high_ref, low_ref, *outs):
    home = home_ref[...]
    total = jnp.dot(high_ref[...], home, preferred_element_type=F32)
    total = total + jnp.dot(low_ref[...], home, preferred_element_type=F32)
    start = 0
    for out in outs:
        rows = out.shape[0]
        out[...] = total[start : start + rows, :].astype(out.dtype)
        start += rows


def per_device(tokens, expert_ids, gate_fixed, w_gate, w_up, w_down):
    col_count = lax.axis_size("expert")
    dp_count = lax.axis_size("dp")
    planes = col_count // 2
    half = planes // 2
    rows, width = tokens.shape
    chunk = half * rows
    slots = 3 * chunk // 32
    sent = dp_count * slots
    plane = (lax.axis_index("expert") // 2).astype(jnp.int32).reshape(1)

    def along_z(x, by):
        return lax.ppermute(
            x, "expert", [(i, (i + 2 * by) % col_count) for i in range(col_count)]
        )

    def partner(x):
        return lax.ppermute(x, "expert", [(i, i ^ 1) for i in range(col_count)])

    def exchange(x):
        return lax.all_to_all(x, "dp", split_axis=0, concat_axis=0, tiled=True)

    pieces = sent // PIECE
    moved = ((sent, width), BF16)

    def dispatch(shards):
        return kernel_call(
            functools.partial(dispatch_kernel, slots, planes),
            "dispatch",
            [moved, ((chunk, EXTRA), BF16)],
            [on_chip(x) for x in shards],
            [plane],
            keep=[pltpu.HBM],
            out_specs=[HBM, VMEM],
            scratch=[pltpu.VMEM(*moved), pltpu.SemaphoreType.DMA((pieces,))],
        )

    def mixing(extra):
        return kernel_call(
            functools.partial(weights_kernel, slots, planes),
            "mixing",
            [((chunk, sent), BF16)] * 2,
            [extra],
            [plane],
            keep=[pltpu.HBM] * 2,
        )

    panels = []
    for w in (w_gate[0], w_up[0], w_down[0]):
        panels += [w, partner(w)]
    g0, g1, u0, u1, d0, d1 = panels

    def expert(x):
        return kernel_call(
            expert_kernel,
            "expert",
            [moved],
            [x] + [off_chip(w) for w in (g0, u0, g1, u1, d0, d1)],
            keep=[pltpu.HBM],
            specs=[VMEM] + [HBM] * 6,
            out_specs=[HBM],
            scratch=[
                pltpu.VMEM((g0.shape[0], 4 * g0.shape[1]), BF16),
                pltpu.VMEM((2 * d0.shape[0], d0.shape[1]), BF16),
                pltpu.VMEM(*moved),
                pltpu.SemaphoreType.DMA((6,)),
                pltpu.SemaphoreType.DMA((pieces,)),
            ],
        )[0]

    def combine(home, mix, kinds):
        outs = [((rows, width), kind) for kind in kinds]
        return kernel_call(combine_kernel, "combine", outs, [home] + [off_chip(m) for m in mix], keep=[pltpu.VMEM] * 4)

    def plus(x, part):
        return (x.astype(F32) + part).astype(BF16)

    mine = kernel_call(
        pack_kernel,
        "pack",
        [((rows, width + EXTRA), BF16)],
        [off_chip(x) for x in (tokens, expert_ids.T, gate_fixed.T)],
        keep=[pltpu.VMEM],
    )[0]
    low_1, high_1 = along_z(mine, 1), along_z(mine, -1)
    low_2, high_2 = along_z(low_1, 1), along_z(high_1, -1)
    low_3, high_3 = along_z(low_2, 1), along_z(high_2, -1)
    low_4 = along_z(low_3, 1)

    near_rows, near_extra = dispatch([mine, low_1, high_1, low_2])
    near = off_chip(exchange(after(near_rows, high_2)))
    far_rows, far_extra = dispatch([high_2, low_3, high_3, low_4])
    near = after(near, far_rows)
    far = exchange(far_rows)
    near_out = after(expert(near), far)
    near_mix, far_mix = mixing(near_extra), mixing(far_extra)
    far_out = after(expert(far), near_out, *near_mix, *far_mix)
    far_home = exchange(far_out)
    near_home = exchange(after(near_out, far_home))
    to_high_2, to_low_3, to_high_3, to_low_4 = combine(far_home, far_mix, [F32, F32, BF16, BF16])
    down, up = along_z(to_low_4, -1), along_z(to_high_3, 1)
    down, up = along_z(plus(down, to_low_3), -1), along_z(plus(up, to_high_2), 1)
    near_home = after(near_home, down, up)
    own, to_low_1, to_high_1, to_low_2 = combine(near_home, near_mix, [F32] * 4)
    down, up = along_z(plus(down, to_low_2), -1), along_z(plus(up, to_high_1), 1)
    down = along_z(plus(down, to_low_1), -1)
    return own + up.astype(F32) + down.astype(F32)


def solution(mesh):
    rows = P(("dp", "expert"), None)
    panels = P(("dp", "expert"), None, None)
    return jax.shard_map(
        per_device,
        mesh=mesh,
        in_specs=(rows, rows, rows, panels, panels, panels),
        out_specs=rows,
        check_vma=False,
    )
```

```python
import functools

import jax
import jax.numpy as jnp
from jax import lax
from jax.experimental import pallas as pl
from jax.experimental.pallas import tpu as pltpu
from jax.sharding import PartitionSpec as P

F32 = jnp.float32
BF16 = jnp.bfloat16
EXTRA = 128
VMEM = pl.BlockSpec(memory_space=pltpu.VMEM)
SMEM = pl.BlockSpec(memory_space=pltpu.SMEM)
HBM = pl.BlockSpec(memory_space=pltpu.HBM)
PIECE = 128
PARAMS = pltpu.CompilerParams(vmem_limit_bytes=24 << 20)


def on_chip(x):
    return pltpu.with_memory_space_constraint(x, pltpu.VMEM)


def off_chip(x):
    return pltpu.with_memory_space_constraint(x, pltpu.HBM)


def after(x, *others):
    return lax.optimization_barrier((x,) + others)[0]


def kernel_call(
    body, name, outs, arrays, scalars=(), keep=(), specs=None, out_specs=None, scratch=()
):
    keep = list(keep) + [jax.ShapeDtypeStruct] * (len(outs) - len(keep))
    return pl.pallas_call(
        body,
        out_shape=[where(*out) for where, out in zip(keep, outs)],
        in_specs=[SMEM] * len(scalars) + (specs or [VMEM] * len(arrays)),
        out_specs=out_specs or [VMEM] * len(outs),
        scratch_shapes=list(scratch),
        compiler_params=PARAMS,
        name=name,
    )(*scalars, *arrays)


def slot_of(index, slots):
    group = jnp.zeros_like(index)
    for d in range(1, 16):
        group = group + (index >= d * slots).astype(jnp.int32)
    return group, index - group * slots


def pack_kernel(tokens_ref, ids_ref, gates_ref, out_ref):
    rows, width = tokens_ref.shape
    gates = gates_ref[...]
    columns = [ids_ref[...], gates >> 8, gates & 255]
    top = jnp.concatenate(columns, axis=0).astype(F32)
    top = jnp.concatenate([top, jnp.zeros((top.shape[0], EXTRA - rows), F32)], axis=1)
    extra = jnp.concatenate([top, jnp.zeros((EXTRA - top.shape[0], EXTRA), F32)], axis=0).T
    out_ref[:, :width] = tokens_ref[...]
    out_ref[:, width:] = extra[:rows, :].astype(BF16)


def dispatch_kernel(slots, planes, z_ref, *refs):
    refs, (out_ref, extra_ref, piece_ref, sems) = refs[:-4], refs[-4:]
    width = out_ref.shape[1]
    groups = out_ref.shape[0] // slots
    extra = jnp.concatenate([x[:, width:] for x in refs], axis=0)
    extra_ref[...] = extra
    extra = extra.astype(F32).T
    tokens = extra.shape[1]
    dest = planes * lax.broadcasted_iota(jnp.int32, (groups, 1), 0) + z_ref[0]
    dest = dest.astype(F32)
    match = jnp.zeros((groups, tokens), F32)
    for k in range(8):
        match = match + (extra[k : k + 1, :] == dest).astype(F32)
    upper = lax.broadcasted_iota(jnp.int32, (tokens, tokens), 0) <= lax.broadcasted_iota(
        jnp.int32, (tokens, tokens), 1
    )
    upper = upper.astype(F32).astype(BF16)
    order = jnp.dot(match.astype(BF16), upper, preferred_element_type=F32) * match
    row = lax.broadcasted_iota(jnp.int32, (groups * slots, 1), 0)
    group, place = slot_of(row, slots)
    spread = (group == lax.broadcasted_iota(jnp.int32, (1, groups), 1)).astype(F32).astype(BF16)
    wanted = jnp.dot(spread, order.astype(BF16), preferred_element_type=F32)
    pick = (wanted == (place + 1).astype(F32)).astype(F32).astype(BF16)
    rows = jnp.concatenate([x[:, :width] for x in refs], axis=0)
    copies = []
    for i in range(out_ref.shape[0] // PIECE):
        here = pl.ds(i * PIECE, PIECE)
        part = pick[i * PIECE : (i + 1) * PIECE, :]
        piece_ref[here, :] = jnp.dot(part, rows, preferred_element_type=F32).astype(BF16)
        copies.append(pltpu.make_async_copy(piece_ref.at[here], out_ref.at[here], sems.at[i]))
        copies[-1].start()
    for copy in copies:
        copy.wait()


def expert_kernel(x_ref, g0, u0, g1, u1, d0, d1, out_hbm, wide, tall, out_ref, sems, out_sems):
    units = g0.shape[1]
    ends = [(w, wide.at[:, pl.ds(i * units, units)]) for i, w in enumerate((g0, u0, g1, u1))]
    ends += [(w, tall.at[pl.ds(i * units, units)]) for i, w in enumerate((d0, d1))]
    loads = [pltpu.make_async_copy(a, b, sems.at[i]) for i, (a, b) in enumerate(ends)]
    for load in loads:
        load.start()
    x = x_ref[...]
    hidden = []
    for i in (0, 2):
        loads[i].wait()
        loads[i + 1].wait()
        both = jnp.dot(
            x, wide[:, i * units : (i + 2) * units], preferred_element_type=F32
        )
        gate, up = both[:, :units], both[:, units:]
        hidden.append((gate / (1.0 + jnp.exp(-gate)) * up).astype(BF16))
    hidden = jnp.concatenate(hidden, axis=1)
    loads[4].wait()
    loads[5].wait()
    copies = []
    for i in range(out_ref.shape[0] // PIECE):
        here = pl.ds(i * PIECE, PIECE)
        total = jnp.dot(
            hidden[i * PIECE : (i + 1) * PIECE, :], tall[...], preferred_element_type=F32
        )
        out_ref[here, :] = total.astype(BF16)
        copies.append(pltpu.make_async_copy(out_ref.at[here], out_hbm.at[here], out_sems.at[i]))
        copies[-1].start()
    for copy in copies:
        copy.wait()


def weights_kernel(slots, planes, z_ref, extra_ref, out_ref):
    tokens, columns = extra_ref.shape[0], out_ref.shape[1]
    groups = columns // slots
    extra = extra_ref[...].astype(F32)
    gates = extra[:, 8:16] * 256.0 + extra[:, 16:24]
    mix = gates / jnp.sum(gates, axis=1, keepdims=True)
    dest = planes * lax.broadcasted_iota(jnp.int32, (1, EXTRA), 1) + z_ref[0]
    dest = dest.astype(F32)
    match = jnp.zeros((tokens, EXTRA), F32)
    weight = jnp.zeros((tokens, EXTRA), F32)
    for k in range(8):
        same = extra[:, k : k + 1] == dest
        match = match + same.astype(F32)
        weight = weight + jnp.where(same, mix[:, k : k + 1], 0.0)
    lower = lax.broadcasted_iota(jnp.int32, (tokens, tokens), 1) <= lax.broadcasted_iota(
        jnp.int32, (tokens, tokens), 0
    )
    lower = lower.astype(F32).astype(BF16)
    order = jnp.dot(lower, match.astype(BF16), preferred_element_type=F32) * match
    column = lax.broadcasted_iota(jnp.int32, (1, groups * slots), 1)
    group, place = slot_of(column, slots)
    spread = (group == lax.broadcasted_iota(jnp.int32, (EXTRA, 1), 0)).astype(F32).astype(BF16)
    wanted = jnp.dot(order.astype(BF16), spread, preferred_element_type=F32)
    here = wanted == (place + 1).astype(F32)
    high = weight.astype(BF16)
    low = (weight - high.astype(F32)).astype(BF16)
    for i, piece in enumerate((high, low)):
        wide = jnp.dot(piece, spread, preferred_element_type=F32)
        out_ref[pl.ds(i * tokens, tokens), :] = jnp.where(here, wide, 0.0).astype(BF16)


def combine_kernel(home_ref, mix_ref, *outs):
    tokens = mix_ref.shape[0] // 2
    total = jnp.dot(mix_ref[...], home_ref[...], preferred_element_type=F32)
    total = total[:tokens, :] + total[tokens:, :]
    start = 0
    for out in outs:
        rows = out.shape[0]
        out[...] = total[start : start + rows, :].astype(out.dtype)
        start += rows


def per_device(tokens, expert_ids, gate_fixed, w_gate, w_up, w_down):
    col_count = lax.axis_size("expert")
    dp_count = lax.axis_size("dp")
    planes = col_count // 2
    half = planes // 2
    rows, width = tokens.shape
    chunk = half * rows
    slots = 3 * chunk // 32
    sent = dp_count * slots
    plane = (lax.axis_index("expert") // 2).astype(jnp.int32).reshape(1)

    def along_z(x, by):
        return lax.ppermute(
            x, "expert", [(i, (i + 2 * by) % col_count) for i in range(col_count)]
        )

    def partner(x):
        return lax.ppermute(x, "expert", [(i, i ^ 1) for i in range(col_count)])

    def exchange(x):
        return lax.all_to_all(x, "dp", split_axis=0, concat_axis=0, tiled=True)

    pieces = sent // PIECE
    moved = ((sent, width), BF16)

    def dispatch(shards):
        return kernel_call(
            functools.partial(dispatch_kernel, slots, planes),
            "dispatch",
            [moved, ((chunk, EXTRA), BF16)],
            [on_chip(x) for x in shards],
            [plane],
            keep=[pltpu.HBM],
            out_specs=[HBM, VMEM],
            scratch=[pltpu.VMEM(*moved), pltpu.SemaphoreType.DMA((pieces,))],
        )

    def mixing(extra):
        return kernel_call(
            functools.partial(weights_kernel, slots, planes),
            "mixing",
            [((2 * chunk, sent), BF16)],
            [extra],
            [plane],
            keep=[pltpu.HBM],
        )[0]

    panels = []
    for w in (w_gate[0], w_up[0], w_down[0]):
        panels += [w, partner(w)]
    g0, g1, u0, u1, d0, d1 = panels

    def expert(x):
        return kernel_call(
            expert_kernel,
            "expert",
            [moved],
            [x] + [off_chip(w) for w in (g0, u0, g1, u1, d0, d1)],
            keep=[pltpu.HBM],
            specs=[VMEM] + [HBM] * 6,
            out_specs=[HBM],
            scratch=[
                pltpu.VMEM((g0.shape[0], 4 * g0.shape[1]), BF16),
                pltpu.VMEM((2 * d0.shape[0], d0.shape[1]), BF16),
                pltpu.VMEM(*moved),
                pltpu.SemaphoreType.DMA((6,)),
                pltpu.SemaphoreType.DMA((pieces,)),
            ],
        )[0]

    def combine(home, mix, kinds):
        outs = [((rows, width), kind) for kind in kinds]
        return kernel_call(combine_kernel, "combine", outs, [home, mix], keep=[pltpu.VMEM] * 4)

    def plus(x, part):
        return (x.astype(F32) + part).astype(BF16)

    mine = kernel_call(
        pack_kernel,
        "pack",
        [((rows, width + EXTRA), BF16)],
        [off_chip(x) for x in (tokens, expert_ids.T, gate_fixed.T)],
        keep=[pltpu.VMEM],
    )[0]
    low_1, high_1 = along_z(mine, 1), along_z(mine, -1)
    low_2, high_2 = along_z(low_1, 1), along_z(high_1, -1)
    low_3, high_3 = along_z(low_2, 1), along_z(high_2, -1)
    low_4 = along_z(low_3, 1)

    near_rows, near_extra = dispatch([mine, low_1, high_1, low_2])
    near = off_chip(exchange(after(near_rows, high_2)))
    far_rows, far_extra = dispatch([high_2, low_3, high_3, low_4])
    near = after(near, far_rows)
    far = exchange(far_rows)
    near_out = after(expert(near), far)
    near_mix, far_mix = mixing(near_extra), mixing(far_extra)
    far_out = after(expert(far), near_out, near_mix, far_mix)
    far_home = exchange(far_out)
    near_home = exchange(after(near_out, far_home))
    to_high_2, to_low_3, to_high_3, to_low_4 = combine(far_home, off_chip(far_mix), [F32, F32, BF16, BF16])
    down, up = along_z(to_low_4, -1), along_z(to_high_3, 1)
    down, up = along_z(plus(down, to_low_3), -1), along_z(plus(up, to_high_2), 1)
    near_home = after(near_home, down, up)
    own, to_low_1, to_high_1, to_low_2 = combine(near_home, off_chip(near_mix), [F32] * 4)
    down, up = along_z(plus(down, to_low_2), -1), along_z(plus(up, to_high_1), 1)
    down = along_z(plus(down, to_low_1), -1)
    return own + up.astype(F32) + down.astype(F32)


def solution(mesh):
    rows = P(("dp", "expert"), None)
    panels = P(("dp", "expert"), None, None)
    return jax.shard_map(
        per_device,
        mesh=mesh,
        in_specs=(rows, rows, rows, panels, panels, panels),
        out_specs=rows,
        check_vma=False,
    )
```

```python
import functools

import jax
import jax.numpy as jnp
from jax import lax
from jax.experimental import pallas as pl
from jax.experimental.pallas import tpu as pltpu
from jax.sharding import PartitionSpec as P

F32 = jnp.float32
BF16 = jnp.bfloat16
EXTRA = 128
VMEM = pl.BlockSpec(memory_space=pltpu.VMEM)
SMEM = pl.BlockSpec(memory_space=pltpu.SMEM)
HBM = pl.BlockSpec(memory_space=pltpu.HBM)
PIECE = 128
PARAMS = pltpu.CompilerParams(vmem_limit_bytes=24 << 20)


def on_chip(x):
    return pltpu.with_memory_space_constraint(x, pltpu.VMEM)


def off_chip(x):
    return pltpu.with_memory_space_constraint(x, pltpu.HBM)


def after(x, *others):
    return lax.optimization_barrier((x,) + others)[0]


def kernel_call(
    body, name, outs, arrays, scalars=(), keep=(), specs=None, out_specs=None, scratch=()
):
    keep = list(keep) + [jax.ShapeDtypeStruct] * (len(outs) - len(keep))
    return pl.pallas_call(
        body,
        out_shape=[where(*out) for where, out in zip(keep, outs)],
        in_specs=[SMEM] * len(scalars) + (specs or [VMEM] * len(arrays)),
        out_specs=out_specs or [VMEM] * len(outs),
        scratch_shapes=list(scratch),
        compiler_params=PARAMS,
        name=name,
    )(*scalars, *arrays)


def slot_of(index, slots):
    group = jnp.zeros_like(index)
    for d in range(1, 16):
        group = group + (index >= d * slots).astype(jnp.int32)
    return group, index - group * slots


def pack_kernel(tokens_ref, ids_ref, gates_ref, out_ref):
    rows, width = tokens_ref.shape
    gates = gates_ref[...]
    columns = [ids_ref[...], gates >> 8, gates & 255]
    top = jnp.concatenate(columns, axis=0).astype(F32)
    top = jnp.concatenate([top, jnp.zeros((top.shape[0], EXTRA - rows), F32)], axis=1)
    extra = jnp.concatenate([top, jnp.zeros((EXTRA - top.shape[0], EXTRA), F32)], axis=0).T
    out_ref[:, :width] = tokens_ref[...]
    out_ref[:, width:] = extra[:rows, :].astype(BF16)


def dispatch_kernel(slots, planes, z_ref, *refs):
    refs, (out_ref, extra_ref, piece_ref, sems) = refs[:-4], refs[-4:]
    width = out_ref.shape[1]
    groups = out_ref.shape[0] // slots
    extra = jnp.concatenate([x[:, width:] for x in refs], axis=0)
    extra_ref[...] = extra
    extra = extra.astype(F32).T
    tokens = extra.shape[1]
    dest = planes * lax.broadcasted_iota(jnp.int32, (groups, 1), 0) + z_ref[0]
    dest = dest.astype(F32)
    match = jnp.zeros((groups, tokens), F32)
    for k in range(8):
        match = match + (extra[k : k + 1, :] == dest).astype(F32)
    upper = lax.broadcasted_iota(jnp.int32, (tokens, tokens), 0) <= lax.broadcasted_iota(
        jnp.int32, (tokens, tokens), 1
    )
    upper = upper.astype(F32).astype(BF16)
    order = jnp.dot(match.astype(BF16), upper, preferred_element_type=F32) * match
    row = lax.broadcasted_iota(jnp.int32, (groups * slots, 1), 0)
    group, place = slot_of(row, slots)
    spread = (group == lax.broadcasted_iota(jnp.int32, (1, groups), 1)).astype(F32).astype(BF16)
    wanted = jnp.dot(spread, order.astype(BF16), preferred_element_type=F32)
    pick = (wanted == (place + 1).astype(F32)).astype(F32).astype(BF16)
    rows = jnp.concatenate([x[:, :width] for x in refs], axis=0)
    copies = []
    for i in range(out_ref.shape[0] // PIECE):
        here = pl.ds(i * PIECE, PIECE)
        part = pick[i * PIECE : (i + 1) * PIECE, :]
        piece_ref[here, :] = jnp.dot(part, rows, preferred_element_type=F32).astype(BF16)
        copies.append(pltpu.make_async_copy(piece_ref.at[here], out_ref.at[here], sems.at[i]))
        copies[-1].start()
    for copy in copies:
        copy.wait()


def expert_kernel(x_ref, g0, u0, g1, u1, d0, d1, out_hbm, wide, tall, out_ref, sems, out_sems):
    units = g0.shape[1]
    ends = [(w, wide.at[:, pl.ds(i * units, units)]) for i, w in enumerate((g0, u0, g1, u1))]
    ends += [(w, tall.at[pl.ds(i * units, units)]) for i, w in enumerate((d0, d1))]
    loads = [pltpu.make_async_copy(a, b, sems.at[i]) for i, (a, b) in enumerate(ends)]
    for load in loads:
        load.start()
    x = x_ref[...]
    hidden = []
    for i in (0, 2):
        loads[i].wait()
        loads[i + 1].wait()
        both = jnp.dot(
            x, wide[:, i * units : (i + 2) * units], preferred_element_type=F32
        )
        gate, up = both[:, :units], both[:, units:]
        hidden.append((gate / (1.0 + jnp.exp(-gate)) * up).astype(BF16))
    hidden = jnp.concatenate(hidden, axis=1)
    loads[4].wait()
    loads[5].wait()
    copies = []
    for i in range(out_ref.shape[0] // PIECE):
        here = pl.ds(i * PIECE, PIECE)
        total = jnp.dot(
            hidden[i * PIECE : (i + 1) * PIECE, :], tall[...], preferred_element_type=F32
        )
        out_ref[here, :] = total.astype(BF16)
        copies.append(pltpu.make_async_copy(out_ref.at[here], out_hbm.at[here], out_sems.at[i]))
        copies[-1].start()
    for copy in copies:
        copy.wait()


def weights_kernel(slots, planes, z_ref, extra_ref, out_ref):
    tokens, columns = extra_ref.shape[0], out_ref.shape[1]
    groups = columns // slots
    extra = extra_ref[...].astype(F32)
    gates = extra[:, 8:16] * 256.0 + extra[:, 16:24]
    mix = gates / jnp.sum(gates, axis=1, keepdims=True)
    dest = planes * lax.broadcasted_iota(jnp.int32, (1, EXTRA), 1) + z_ref[0]
    dest = dest.astype(F32)
    match = jnp.zeros((tokens, EXTRA), F32)
    weight = jnp.zeros((tokens, EXTRA), F32)
    for k in range(8):
        same = extra[:, k : k + 1] == dest
        match = match + same.astype(F32)
        weight = weight + jnp.where(same, mix[:, k : k + 1], 0.0)
    lower = lax.broadcasted_iota(jnp.int32, (tokens, tokens), 1) <= lax.broadcasted_iota(
        jnp.int32, (tokens, tokens), 0
    )
    lower = lower.astype(F32).astype(BF16)
    order = jnp.dot(lower, match.astype(BF16), preferred_element_type=F32) * match
    column = lax.broadcasted_iota(jnp.int32, (1, groups * slots), 1)
    group, place = slot_of(column, slots)
    spread = (group == lax.broadcasted_iota(jnp.int32, (EXTRA, 1), 0)).astype(F32).astype(BF16)
    wanted = jnp.dot(order.astype(BF16), spread, preferred_element_type=F32)
    here = wanted == (place + 1).astype(F32)
    high = weight.astype(BF16)
    low = (weight - high.astype(F32)).astype(BF16)
    for i, piece in enumerate((high, low)):
        wide = jnp.dot(piece, spread, preferred_element_type=F32)
        out_ref[pl.ds(i * tokens, tokens), :] = jnp.where(here, wide, 0.0).astype(BF16)


def combine_kernel(home_ref, mix_ref, *outs):
    tokens = mix_ref.shape[0] // 2
    total = jnp.dot(mix_ref[...], home_ref[...], preferred_element_type=F32)
    total = total[:tokens, :] + total[tokens:, :]
    start = 0
    for out in outs:
        rows = out.shape[0]
        out[...] = total[start : start + rows, :].astype(out.dtype)
        start += rows


def per_device(tokens, expert_ids, gate_fixed, w_gate, w_up, w_down):
    col_count = lax.axis_size("expert")
    dp_count = lax.axis_size("dp")
    planes = col_count // 2
    half = planes // 2
    rows, width = tokens.shape
    chunk = half * rows
    slots = 3 * chunk // 32
    sent = dp_count * slots
    plane = (lax.axis_index("expert") // 2).astype(jnp.int32).reshape(1)

    def along_z(x, by):
        return lax.ppermute(
            x, "expert", [(i, (i + 2 * by) % col_count) for i in range(col_count)]
        )

    def partner(x):
        return lax.ppermute(x, "expert", [(i, i ^ 1) for i in range(col_count)])

    def exchange(x):
        return lax.all_to_all(x, "dp", split_axis=0, concat_axis=0, tiled=True)

    pieces = sent // PIECE
    moved = ((sent, width), BF16)

    def dispatch(shards):
        return kernel_call(
            functools.partial(dispatch_kernel, slots, planes),
            "dispatch",
            [moved, ((chunk, EXTRA), BF16)],
            [on_chip(x) for x in shards],
            [plane],
            keep=[pltpu.HBM],
            out_specs=[HBM, VMEM],
            scratch=[pltpu.VMEM(*moved), pltpu.SemaphoreType.DMA((pieces,))],
        )

    def mixing(extra, where):
        return kernel_call(
            functools.partial(weights_kernel, slots, planes),
            "mixing",
            [((2 * chunk, sent), BF16)],
            [extra],
            [plane],
            keep=[where],
        )[0]

    panels = []
    for w in (w_gate[0], w_up[0], w_down[0]):
        panels += [w, partner(w)]
    g0, g1, u0, u1, d0, d1 = panels

    def expert(x):
        return kernel_call(
            expert_kernel,
            "expert",
            [moved],
            [x] + [off_chip(w) for w in (g0, u0, g1, u1, d0, d1)],
            keep=[pltpu.HBM],
            specs=[VMEM] + [HBM] * 6,
            out_specs=[HBM],
            scratch=[
                pltpu.VMEM((g0.shape[0], 4 * g0.shape[1]), BF16),
                pltpu.VMEM((2 * d0.shape[0], d0.shape[1]), BF16),
                pltpu.VMEM(*moved),
                pltpu.SemaphoreType.DMA((6,)),
                pltpu.SemaphoreType.DMA((pieces,)),
            ],
        )[0]

    def combine(home, mix, kinds):
        outs = [((rows, width), kind) for kind in kinds]
        return kernel_call(combine_kernel, "combine", outs, [home, mix], keep=[pltpu.VMEM] * 4)

    def plus(x, part):
        return (x.astype(F32) + part).astype(BF16)

    mine = kernel_call(
        pack_kernel,
        "pack",
        [((rows, width + EXTRA), BF16)],
        [off_chip(x) for x in (tokens, expert_ids.T, gate_fixed.T)],
        keep=[pltpu.VMEM],
    )[0]
    low_1, high_1 = along_z(mine, 1), along_z(mine, -1)
    low_2, high_2 = along_z(low_1, 1), along_z(high_1, -1)
    low_3, high_3 = along_z(low_2, 1), along_z(high_2, -1)
    low_4 = along_z(low_3, 1)

    near_rows, near_extra = dispatch([mine, low_1, high_1, low_2])
    near = off_chip(exchange(after(near_rows, high_2)))
    far_rows, far_extra = dispatch([high_2, low_3, high_3, low_4])
    near = after(near, far_rows)
    far = exchange(far_rows)
    near_out = after(expert(near), far)
    far_mix = mixing(far_extra, pltpu.HBM)
    far_out = after(expert(far), near_out, far_mix)
    far_home = exchange(far_out)
    near_mix = mixing(after(near_extra, far_home), pltpu.VMEM)
    near_home = exchange(after(near_out, far_home))
    to_high_2, to_low_3, to_high_3, to_low_4 = combine(far_home, off_chip(far_mix), [F32, F32, BF16, BF16])
    down, up = along_z(to_low_4, -1), along_z(to_high_3, 1)
    down, up = along_z(plus(down, to_low_3), -1), along_z(plus(up, to_high_2), 1)
    near_home = after(near_home, down, up)
    own, to_low_1, to_high_1, to_low_2 = combine(near_home, near_mix, [F32] * 4)
    down, up = along_z(plus(down, to_low_2), -1), along_z(plus(up, to_high_1), 1)
    down = along_z(plus(down, to_low_1), -1)
    return own + up.astype(F32) + down.astype(F32)


def solution(mesh):
    rows = P(("dp", "expert"), None)
    panels = P(("dp", "expert"), None, None)
    return jax.shard_map(
        per_device,
        mesh=mesh,
        in_specs=(rows, rows, rows, panels, panels, panels),
        out_specs=rows,
        check_vma=False,
    )
```

```python
import functools

import jax
import jax.numpy as jnp
from jax import lax
from jax.experimental import pallas as pl
from jax.experimental.pallas import tpu as pltpu
from jax.sharding import PartitionSpec as P

F32 = jnp.float32
BF16 = jnp.bfloat16
EXTRA = 128
VMEM = pl.BlockSpec(memory_space=pltpu.VMEM)
SMEM = pl.BlockSpec(memory_space=pltpu.SMEM)
HBM = pl.BlockSpec(memory_space=pltpu.HBM)
PIECE = 128
PARAMS = pltpu.CompilerParams(vmem_limit_bytes=24 << 20)


def on_chip(x):
    return pltpu.with_memory_space_constraint(x, pltpu.VMEM)


def off_chip(x):
    return pltpu.with_memory_space_constraint(x, pltpu.HBM)


def after(x, *others):
    return lax.optimization_barrier((x,) + others)[0]


def kernel_call(
    body, name, outs, arrays, scalars=(), keep=(), specs=None, out_specs=None, scratch=()
):
    keep = list(keep) + [jax.ShapeDtypeStruct] * (len(outs) - len(keep))
    return pl.pallas_call(
        body,
        out_shape=[where(*out) for where, out in zip(keep, outs)],
        in_specs=[SMEM] * len(scalars) + (specs or [VMEM] * len(arrays)),
        out_specs=out_specs or [VMEM] * len(outs),
        scratch_shapes=list(scratch),
        compiler_params=PARAMS,
        name=name,
    )(*scalars, *arrays)


def slot_of(index, slots):
    group = jnp.zeros_like(index)
    for d in range(1, 16):
        group = group + (index >= d * slots).astype(jnp.int32)
    return group, index - group * slots


def pack_kernel(tokens_ref, ids_ref, gates_ref, out_ref):
    rows, width = tokens_ref.shape
    gates = gates_ref[...]
    columns = [ids_ref[...], gates >> 8, gates & 255]
    top = jnp.concatenate(columns, axis=0).astype(F32)
    top = jnp.concatenate([top, jnp.zeros((top.shape[0], EXTRA - rows), F32)], axis=1)
    extra = jnp.concatenate([top, jnp.zeros((EXTRA - top.shape[0], EXTRA), F32)], axis=0).T
    out_ref[:, :width] = tokens_ref[...]
    out_ref[:, width:] = extra[:rows, :].astype(BF16)


def dispatch_kernel(slots, planes, z_ref, *refs):
    refs, (out_ref, extra_ref, piece_ref, sems) = refs[:-4], refs[-4:]
    width = out_ref.shape[1]
    groups = out_ref.shape[0] // slots
    extra = jnp.concatenate([x[:, width:] for x in refs], axis=0)
    extra_ref[...] = extra
    extra = extra.astype(F32).T
    tokens = extra.shape[1]
    dest = planes * lax.broadcasted_iota(jnp.int32, (groups, 1), 0) + z_ref[0]
    dest = dest.astype(F32)
    match = jnp.zeros((groups, tokens), F32)
    for k in range(8):
        match = match + (extra[k : k + 1, :] == dest).astype(F32)
    upper = lax.broadcasted_iota(jnp.int32, (tokens, tokens), 0) <= lax.broadcasted_iota(
        jnp.int32, (tokens, tokens), 1
    )
    upper = upper.astype(F32).astype(BF16)
    order = jnp.dot(match.astype(BF16), upper, preferred_element_type=F32) * match
    row = lax.broadcasted_iota(jnp.int32, (groups * slots, 1), 0)
    group, place = slot_of(row, slots)
    spread = (group == lax.broadcasted_iota(jnp.int32, (1, groups), 1)).astype(F32).astype(BF16)
    wanted = jnp.dot(spread, order.astype(BF16), preferred_element_type=F32)
    pick = (wanted == (place + 1).astype(F32)).astype(F32).astype(BF16)
    rows = jnp.concatenate([x[:, :width] for x in refs], axis=0)
    copies = []
    for i in range(out_ref.shape[0] // PIECE):
        here = pl.ds(i * PIECE, PIECE)
        part = pick[i * PIECE : (i + 1) * PIECE, :]
        piece_ref[here, :] = jnp.dot(part, rows, preferred_element_type=F32).astype(BF16)
        copies.append(pltpu.make_async_copy(piece_ref.at[here], out_ref.at[here], sems.at[i]))
        copies[-1].start()
    for copy in copies:
        copy.wait()


def expert_kernel(x_ref, g0, u0, g1, u1, d0, d1, out_hbm, wide, tall, out_ref, sems, out_sems):
    units = g0.shape[1]
    ends = [(w, wide.at[:, pl.ds(i * units, units)]) for i, w in enumerate((g0, u0, g1, u1))]
    ends += [(w, tall.at[pl.ds(i * units, units)]) for i, w in enumerate((d0, d1))]
    loads = [pltpu.make_async_copy(a, b, sems.at[i]) for i, (a, b) in enumerate(ends)]
    for load in loads:
        load.start()
    x = x_ref[...]
    hidden = []
    for i in (0, 2):
        loads[i].wait()
        loads[i + 1].wait()
        both = jnp.dot(
            x, wide[:, i * units : (i + 2) * units], preferred_element_type=F32
        )
        gate, up = both[:, :units], both[:, units:]
        hidden.append((gate / (1.0 + jnp.exp(-gate)) * up).astype(BF16))
    hidden = jnp.concatenate(hidden, axis=1)
    loads[4].wait()
    loads[5].wait()
    copies = []
    for i in range(out_ref.shape[0] // PIECE):
        here = pl.ds(i * PIECE, PIECE)
        total = jnp.dot(
            hidden[i * PIECE : (i + 1) * PIECE, :], tall[...], preferred_element_type=F32
        )
        out_ref[here, :] = total.astype(BF16)
        copies.append(pltpu.make_async_copy(out_ref.at[here], out_hbm.at[here], out_sems.at[i]))
        copies[-1].start()
    for copy in copies:
        copy.wait()


def weights_kernel(slots, planes, z_ref, extra_ref, out_ref):
    tokens, columns = extra_ref.shape[0], out_ref.shape[1]
    groups = columns // slots
    extra = extra_ref[...].astype(F32)
    gates = extra[:, 8:16] * 256.0 + extra[:, 16:24]
    mix = gates / jnp.sum(gates, axis=1, keepdims=True)
    dest = planes * lax.broadcasted_iota(jnp.int32, (1, EXTRA), 1) + z_ref[0]
    dest = dest.astype(F32)
    match = jnp.zeros((tokens, EXTRA), F32)
    weight = jnp.zeros((tokens, EXTRA), F32)
    for k in range(8):
        same = extra[:, k : k + 1] == dest
        match = match + same.astype(F32)
        weight = weight + jnp.where(same, mix[:, k : k + 1], 0.0)
    lower = lax.broadcasted_iota(jnp.int32, (tokens, tokens), 1) <= lax.broadcasted_iota(
        jnp.int32, (tokens, tokens), 0
    )
    lower = lower.astype(F32).astype(BF16)
    order = jnp.dot(lower, match.astype(BF16), preferred_element_type=F32) * match
    column = lax.broadcasted_iota(jnp.int32, (1, groups * slots), 1)
    group, place = slot_of(column, slots)
    spread = (group == lax.broadcasted_iota(jnp.int32, (EXTRA, 1), 0)).astype(F32).astype(BF16)
    wanted = jnp.dot(order.astype(BF16), spread, preferred_element_type=F32)
    here = wanted == (place + 1).astype(F32)
    high = weight.astype(BF16)
    low = (weight - high.astype(F32)).astype(BF16)
    for i, piece in enumerate((high, low)):
        wide = jnp.dot(piece, spread, preferred_element_type=F32)
        out_ref[pl.ds(i * tokens, tokens), :] = jnp.where(here, wide, 0.0).astype(BF16)


def combine_kernel(home_ref, mix_ref, *outs):
    tokens = mix_ref.shape[0] // 2
    total = jnp.dot(mix_ref[...], home_ref[...], preferred_element_type=F32)
    total = total[:tokens, :] + total[tokens:, :]
    start = 0
    for out in outs:
        rows = out.shape[0]
        out[...] = total[start : start + rows, :].astype(out.dtype)
        start += rows


def per_device(tokens, expert_ids, gate_fixed, w_gate, w_up, w_down):
    col_count = lax.axis_size("expert")
    dp_count = lax.axis_size("dp")
    planes = col_count // 2
    half = planes // 2
    rows, width = tokens.shape
    chunk = half * rows
    slots = 3 * chunk // 32
    sent = dp_count * slots
    plane = (lax.axis_index("expert") // 2).astype(jnp.int32).reshape(1)

    def along_z(x, by):
        return lax.ppermute(
            x, "expert", [(i, (i + 2 * by) % col_count) for i in range(col_count)]
        )

    def partner(x):
        return lax.ppermute(x, "expert", [(i, i ^ 1) for i in range(col_count)])

    def exchange(x):
        return lax.all_to_all(x, "dp", split_axis=0, concat_axis=0, tiled=True)

    pieces = sent // PIECE
    moved = ((sent, width), BF16)

    def dispatch(shards):
        return kernel_call(
            functools.partial(dispatch_kernel, slots, planes),
            "dispatch",
            [moved, ((chunk, EXTRA), BF16)],
            [on_chip(x) for x in shards],
            [plane],
            keep=[pltpu.HBM],
            out_specs=[HBM, VMEM],
            scratch=[pltpu.VMEM(*moved), pltpu.SemaphoreType.DMA((pieces,))],
        )

    def mixing(extra, where):
        return kernel_call(
            functools.partial(weights_kernel, slots, planes),
            "mixing",
            [((2 * chunk, sent), BF16)],
            [extra],
            [plane],
            keep=[where],
        )[0]

    panels = []
    for w in (w_gate[0], w_up[0], w_down[0]):
        panels += [w, partner(w)]
    g0, g1, u0, u1, d0, d1 = panels

    def expert(x):
        return kernel_call(
            expert_kernel,
            "expert",
            [moved],
            [x] + [off_chip(w) for w in (g0, u0, g1, u1, d0, d1)],
            keep=[pltpu.HBM],
            specs=[VMEM] + [HBM] * 6,
            out_specs=[HBM],
            scratch=[
                pltpu.VMEM((g0.shape[0], 4 * g0.shape[1]), BF16),
                pltpu.VMEM((2 * d0.shape[0], d0.shape[1]), BF16),
                pltpu.VMEM(*moved),
                pltpu.SemaphoreType.DMA((6,)),
                pltpu.SemaphoreType.DMA((pieces,)),
            ],
        )[0]

    def combine(home, mix, kinds):
        outs = [((rows, width), kind) for kind in kinds]
        return kernel_call(combine_kernel, "combine", outs, [home, mix], keep=[pltpu.VMEM] * 4)

    def plus(x, part):
        return (x.astype(F32) + part).astype(BF16)

    mine = kernel_call(
        pack_kernel,
        "pack",
        [((rows, width + EXTRA), BF16)],
        [off_chip(x) for x in (tokens, expert_ids.T, gate_fixed.T)],
        keep=[pltpu.VMEM],
    )[0]
    low_1, high_1 = along_z(mine, 1), along_z(mine, -1)
    low_2, high_2 = along_z(low_1, 1), along_z(high_1, -1)
    low_3, high_3 = along_z(low_2, 1), along_z(high_2, -1)
    low_4 = along_z(low_3, 1)

    near_rows, near_extra = dispatch([mine, low_1, high_1, low_2])
    near = off_chip(exchange(after(near_rows, high_2)))
    far_rows, far_extra = dispatch([high_2, low_3, high_3, low_4])
    near = after(near, far_rows)
    far = exchange(far_rows)
    near_out = after(expert(near), far)
    far_mix = mixing(far_extra, pltpu.HBM)
    far_out = after(expert(far), near_out, far_mix)
    far_home = exchange(far_out)
    near_mix = mixing(after(near_extra, far_home), pltpu.VMEM)
    near_home = exchange(after(near_out, far_home))
    to_high_2, to_low_3, to_high_3, to_low_4 = combine(far_home, far_mix, [F32, F32, BF16, BF16])
    down, up = along_z(to_low_4, -1), along_z(to_high_3, 1)
    down, up = along_z(plus(down, to_low_3), -1), along_z(plus(up, to_high_2), 1)
    near_home = after(near_home, down, up)
    own, to_low_1, to_high_1, to_low_2 = combine(near_home, near_mix, [F32] * 4)
    down, up = along_z(plus(down, to_low_2), -1), along_z(plus(up, to_high_1), 1)
    down = along_z(plus(down, to_low_1), -1)
    return own + up.astype(F32) + down.astype(F32)


def solution(mesh):
    rows = P(("dp", "expert"), None)
    panels = P(("dp", "expert"), None, None)
    return jax.shard_map(
        per_device,
        mesh=mesh,
        in_specs=(rows, rows, rows, panels, panels, panels),
        out_specs=rows,
        check_vma=False,
    )
```
